32 devices in a mesh: groups: 2 (over x), visit: 16 (over z, y, core).
Axes of the slice: x: 2, y: 2, z: 4, core: 2. Of those that a mesh axis runs over, the one named last changes fastest.
Arguments:
- science: float32 [8192, 1024], P(('groups', 'visit')), parts along dimension 0, may hold values from -6 to 6
- template: bfloat16 [8192, 1024], P(('groups', 'visit')), parts along dimension 0, may hold values from -6 to 6
- owner_map: int32 [32], P('groups'), parts along dimension 0, may hold values from 0 to 15, as said below
- covering: int32 [32, 4], P(('groups', 'visit')), parts along dimension 0, may hold values from 0 to 15, as said below
- row_shift: int32 [32, 4], P(('groups', 'visit')), parts along dimension 0, may hold values from -128 to 128, as said below
- col_shift: int32 [32, 4], P(('groups', 'visit')), parts along dimension 0, may hold values from -256 to 256, as said below
- basis_cols: float32 [20, 21], replicated, may hold values from -1.25 to 1.25
- basis_rows: float32 [20, 21], replicated, may hold values from -1.25 to 1.25
- coeffs: float32 [8, 20], P('groups'), parts along dimension 0, may hold values from -1.25 to 1.25
- psf_kernel: float32 [9, 9], replicated, may hold values from 0 to 0.25
Outputs:
- difference: float32 [8192, 1024], P(('groups', 'visit')), parts along dimension 0
- detection: float32 [8192, 1024], P(('groups', 'visit')), parts along dimension 0
The draws below stay inside these ranges and needn't reach their ends.
There are 2 independent parts, one for each index of `groups`. The reference program is written for one: setup_inputs(seed, part) draws one part's arguments, and reference() takes and returns one part's arrays. A program takes and returns all parts, laid end to end along the dimension named above; an argument that names none is the same for every part. Nothing has to cross between parts.
Inputs may be any that keep to these rules, and one draw needn't show every extreme that they name: owner_map is a permutation: every device stores exactly one template piece. `covering`: the 4 pieces listed for a row block are different; the first is the piece stored on that block's own device; every listed piece is stored on a device at most 3 positions away along the visit axis, and on some device exactly 3. `row_shift`: the first slot of every row block has shift 0; both ends of the range are reached. `col_shift`: the first slot of every row block has shift 0; both ends of the range are reached.
All inputs are finite; a program needn't handle non-finite values.
Results may differ from the reference program's by a relative error of at most 0.005.
Values may be sent and summed in bfloat16 or wider, within the bound.
No kernel may reach another device: no remote copies, remote signals or barrier semaphores. Data moves between devices by JAX's collectives and lax.ppermute only.
A program may use at most 64 MiB of HBM per device.

```python
import jax
import jax.numpy as jnp
from jax import lax

NB = 20
KS = 21
RIM = 10
KP = 9
PR = 4
ROWS = 256
COLS = 1024
PIECES = 4
SLOTS = 4
REACH = 3
VISITS = 4
IMAGE_ROWS = 4096
N_VISIT = 16


def layout_draw(key):
    base_key = jax.random.fold_in(key, 71)
    owner_table = jax.random.permutation(jax.random.fold_in(base_key, 1), N_VISIT).astype(jnp.int32)
    stored = jnp.argsort(owner_table, stable=True).astype(jnp.int32)
    device = jnp.arange(N_VISIT, dtype=jnp.int32)
    steps_list = jnp.concatenate([jnp.arange(-REACH, 0, dtype=jnp.int32), jnp.arange(1, REACH + 1, dtype=jnp.int32)])
    target = device[:, None] + steps_list[None, :]
    inside_axis = (target >= 0) & (target < N_VISIT)
    position_rank = jnp.arange(2 * REACH, dtype=jnp.int32)
    raw_score = jax.random.randint(jax.random.fold_in(base_key, 2), (N_VISIT, 2 * REACH), 0, 4096, dtype=jnp.int32)
    scores = jnp.where(inside_axis, raw_score * (2 * REACH) + position_rank[None, :], 4096 * 2 * REACH + position_rank[None, :])
    picked = lax.top_k(-scores, SLOTS - 1)[1]
    chosen = jnp.take_along_axis(target, picked, axis=1)
    devices = jnp.concatenate([device[:, None], chosen], axis=1)
    pieces = stored[devices]
    return (owner_table, pieces.astype(jnp.int32))


def draw_owner_map(key, part):
    return layout_draw(key)[0]


def draw_covering(key, part):
    return layout_draw(key)[1]


def shift_draw(key, limit, salt):
    values = jax.random.randint(jax.random.fold_in(key, salt), (N_VISIT, SLOTS), -limit, limit + 1, dtype=jnp.int32)
    values = values.at[:, 0].set(0)
    chosen = jax.random.randint(jax.random.fold_in(key, salt + 1), (), 0, N_VISIT, dtype=jnp.int32)
    values = values.at[chosen, 1].set(limit)
    values = values.at[chosen, 2].set(-limit)
    return values


def draw_row_shift(key, part):
    return shift_draw(key, ROWS // 2, 81)


def draw_col_shift(key, part):
    return shift_draw(key, COLS // 4, 91)


def block_levels(own_key, extent, cuts, low, largest):
    factor_of = 1.0
    for position, parts in cuts:
        steps = jax.random.uniform(jax.random.fold_in(jax.random.fold_in(own_key, 6), position), (parts,), jnp.float32, low / len(cuts), largest / len(cuts))
        factor_of = factor_of * jnp.repeat(jnp.exp(steps), extent[position] // parts).reshape((-1,) + (1,) * (len(extent) - 1 - position))
    return factor_of


def bell_draw(rng, dims, deviation, reach, cuts=(), kind=jnp.bfloat16):
    values = jax.random.normal(rng, dims, jnp.float32) * deviation
    if len(cuts) > 0:
        values = block_levels(rng, dims, cuts, -0.22, 0.18) * values
    return jnp.clip(values, min=-reach, max=reach).astype(kind)


def setup_inputs(seed: int = 0, part: int = 0) -> dict:
    streams_of = jax.random.split(jax.random.key(seed), 11)
    part_keys = jax.random.split(jax.random.fold_in(streams_of[10], part), 11)
    science = bell_draw(part_keys[0], (IMAGE_ROWS, COLS), 1.0, 6.0, ((0, 16),), jnp.float32)
    template = bell_draw(part_keys[1], (IMAGE_ROWS, COLS), 1.0, 6.0, ((0, 16),))
    owner_map = draw_owner_map(jax.random.fold_in(jax.random.fold_in(streams_of[10], part), 71), part)
    covering = draw_covering(jax.random.fold_in(jax.random.fold_in(streams_of[10], part), 71), part)
    row_shift = draw_row_shift(jax.random.fold_in(jax.random.fold_in(streams_of[10], part), 71), part)
    col_shift = draw_col_shift(jax.random.fold_in(jax.random.fold_in(streams_of[10], part), 71), part)
    basis_cols = bell_draw(streams_of[6], (NB, KS), KS ** -0.5, 1.25, (), jnp.float32)
    basis_rows = bell_draw(streams_of[7], (NB, KS), KS ** -0.5, 1.25, (), jnp.float32)
    coeffs = bell_draw(part_keys[8], (VISITS, NB), NB ** -0.5, 1.25, (), jnp.float32)
    psf_kernel = jnp.clip(jax.random.uniform(streams_of[9], (KP, KP), jnp.float32, 0.0, 0.25), 0.0, 0.25)
    return {"science": science, "template": template, "owner_map": owner_map, "covering": covering, "row_shift": row_shift, "col_shift": col_shift, "basis_cols": basis_cols, "basis_rows": basis_rows, "coeffs": coeffs, "psf_kernel": psf_kernel}


def round_trip(values):
    return lax.optimization_barrier(values.astype(jnp.bfloat16)).astype(jnp.float32)

def place_piece(piece, row_off, col_off):
    half_rows = ROWS // 2
    quarter_cols = COLS // 4
    padded = jnp.pad(piece, ((half_rows, half_rows), (quarter_cols, quarter_cols)))
    start_row = (half_rows - row_off).astype(jnp.int32)
    start_col = (quarter_cols - col_off).astype(jnp.int32)
    return lax.dynamic_slice(padded, (start_row, start_col), (ROWS, COLS))

def reference(science, template, owner_map, covering, row_shift, col_shift, basis_cols, basis_rows, coeffs, psf_kernel):
    stored = template.reshape(N_VISIT, ROWS, COLS)
    ones_piece = jnp.ones((ROWS, COLS), jnp.float32)

    def canvas_of(device):
        placed_sum = jnp.zeros((ROWS, COLS), jnp.float32)
        coverage = jnp.zeros((ROWS, COLS), jnp.float32)
        for slot_index in range(SLOTS):
            holder = owner_map[covering[device, slot_index]].astype(jnp.int32)
            piece = lax.dynamic_index_in_dim(stored, holder, 0, keepdims=False).astype(jnp.float32)
            placed_sum = placed_sum + place_piece(piece, row_shift[device, slot_index], col_shift[device, slot_index])
            coverage = coverage + place_piece(ones_piece, row_shift[device, slot_index], col_shift[device, slot_index])
        return (placed_sum / coverage).astype(jnp.bfloat16)
    canvases = jnp.roll(lax.map(canvas_of, jnp.arange(N_VISIT, dtype=jnp.int32)), 1, axis=0)
    taps_cols = round_trip(basis_cols)
    taps_psf = round_trip(psf_kernel)
    weights_all = round_trip(coeffs[:, :, None] * basis_rows[None, :, :])
    science_visits = jnp.roll(science, ROWS, axis=0).reshape(VISITS, PIECES * ROWS, COLS)
    visit_rows = PIECES * ROWS

    def visit_fn(visit):
        start = (visit * PIECES).astype(jnp.int32)
        image = lax.dynamic_slice_in_dim(canvases, start, PIECES, 0).reshape(visit_rows, COLS).astype(jnp.float32)
        padded = jnp.pad(image, ((RIM, RIM), (RIM, RIM)))
        col_pass = jnp.zeros((NB, visit_rows + 2 * RIM, COLS), jnp.float32)
        for tap_index in range(KS):
            col_pass = col_pass + taps_cols[:, tap_index, None, None] * padded[None, :, tap_index:tap_index + COLS]
        col_pass = round_trip(col_pass)
        weights = lax.dynamic_index_in_dim(weights_all, visit, 0, keepdims=False)
        model_image = jnp.zeros((visit_rows, COLS), jnp.float32)
        for tap_index in range(KS):
            model_image = model_image + jnp.einsum('b,brc->rc', weights[:, tap_index], col_pass[:, tap_index:tap_index + visit_rows], precision=lax.Precision.HIGHEST)
        difference = lax.dynamic_index_in_dim(science_visits, visit, 0, keepdims=False) - model_image
        variance = jnp.mean(difference * difference)
        rounded = jnp.pad(round_trip(difference), ((PR, PR), (PR, PR)))
        response = jnp.zeros((visit_rows, COLS), jnp.float32)
        for row_tap in range(KP):
            for col_tap in range(KP):
                response = response + taps_psf[row_tap, col_tap] * rounded[row_tap:row_tap + visit_rows, col_tap:col_tap + COLS]
        detection = response / jnp.sqrt(variance + 1e-06)
        return (difference, detection)
    differences, detections = lax.map(visit_fn, jnp.arange(VISITS, dtype=jnp.int32))
    differences = jnp.roll(differences.reshape(N_VISIT * ROWS, COLS), -ROWS, axis=0)
    detections = jnp.roll(detections.reshape(N_VISIT * ROWS, COLS), -ROWS, axis=0)
    return (differences, detections)
```

```python
import jax
import jax.numpy as jnp
from jax import lax
from jax.experimental import pallas as pl
from jax.experimental.pallas import tpu as pltpu
from jax.sharding import PartitionSpec as P

PIECES = 4
LANES = 128

BUFFER_OF = ((4, 5, 6, 0, 1, 2, 3), (6, 5, 1, 0, 3, 2, 4), (4, 2, 3, 0, 1, 5, 6), (3, 2, 1, 0, 6, 5, 4))


def gather_pieces(own, position):
    count = lax.axis_size("visit")

    def move(value, pairs):
        kept = [(i, j) for i, j in pairs if 0 <= j < count]
        return lax.ppermute(value, "visit", kept)

    pair = move(own, [(i, i ^ 2) for i in range(count)])
    far = move(own, [(i, i + 3 if i % 2 else i - 3) for i in range(count)])
    partner = move(own, [(i, i ^ 1) for i in range(count)])
    residue = position % 4
    relay = jnp.where((residue == 1) | (residue == 2), far, pair)
    targets = {0: 4, 1: 1, 2: -1, 3: -4}
    relayed = move(relay, [(i, i + targets[i % 4]) for i in range(count)])
    crossed = move(pair, [(i, i ^ 1) for i in range(count)])
    relayed_crossed = move(relayed, [(i, i ^ 1) for i in range(count)])
    return (own, partner, pair, crossed, far, relayed, relayed_crossed)


def canvas_kernel(rim, scalars, rows_hot, recip, *refs):
    pieces, out, moved = refs[:7], refs[7], refs[8]
    rows, cols = pieces[0].shape
    width = out.shape[1]
    tiles = width // LANES
    slots = rows_hot.shape[0]
    before = 3 * LANES
    moved[:, :before] = jnp.zeros((rows, before), jnp.float32)
    moved[:, before + cols :] = jnp.zeros((rows, moved.shape[1] - before - cols), jnp.float32)
    moved[:, before : before + cols] = pieces[0][...].astype(jnp.float32)
    chunk = 16
    lane = lax.broadcasted_iota(jnp.int32, (chunk, LANES), 1)

    def add_shifted(col_shift, final, first):
        offset = before - rim - col_shift
        start = offset // LANES
        left = offset - start * LANES
        turn = lax.rem(LANES - left, LANES)
        keep = lane < LANES - left

        def body(step, carry):
            at = pl.ds(pl.multiple_of(step * chunk, chunk), chunk)
            turned = []
            for k in range(tiles + 1):
                lanes = pl.ds(pl.multiple_of((start + k) * LANES, LANES), LANES)
                turned.append(pltpu.roll(moved[at, lanes], turn, 1))
            for k in range(tiles):
                here = slice(k * LANES, (k + 1) * LANES)
                value = jnp.where(keep, turned[k], turned[k + 1])
                if not first:
                    value = value + out[at, here]
                if final:
                    value = value * recip[at, here]
                out[at, here] = value
            return carry

        lax.fori_loop(0, rows // chunk, body, 0)

    add_shifted(jnp.int32(0) + scalars[0, 0] * 0, False, True)
    for slot in range(slots):
        for index in range(1, 7):

            @pl.when(scalars[0, 1 + slot] == index)
            def _():
                moved[:, before : before + cols] = jnp.dot(
                    rows_hot[slot], pieces[index][...], preferred_element_type=jnp.float32
                )

        add_shifted(scalars[0, 1 + slots + slot], slot == slots - 1, False)


def toeplitz_kernel(taps, reach, bands):
    count = taps.shape[0] if reach is None else reach
    bands[0, :, LANES:] = jnp.zeros((256, LANES), bands.dtype)
    bands[count, :, :LANES] = jnp.zeros((256, LANES), bands.dtype)
    for tap in range(count):
        spread = jnp.broadcast_to(taps[tap : tap + 1, :], (256, 256))
        table = pltpu.roll(spread, 0, 1, stride=1, stride_axis=0)[:, :LANES].astype(bands.dtype)
        bands[tap, :, :LANES] = table
        bands[tap + 1, :, LANES:] = table


def bands_kernel(model_taps, psf_taps, model_bands, psf_bands):
    toeplitz_kernel(model_taps, model_bands.shape[0] - 1, model_bands)
    toeplitz_kernel(psf_taps, psf_bands.shape[0] - 1, psf_bands)


def pair_rows(source, base, offsets, pairs, packed):
    for offset in range(offsets):
        for k in range(source.shape[0]):
            here = slice(k * LANES, (k + 1) * LANES)
            rows = source[k, pl.ds(base + offset, pairs, stride=2), :]
            packed[offset, :, here] = rows.astype(jnp.bfloat16)


def band_product(packed, bands, k):
    left = jnp.concatenate(
        [packed[o, :, k * LANES : k * LANES + 256] for o in range(bands.shape[0])], axis=1
    )
    return jnp.dot(
        left, bands[...].reshape(bands.shape[0] * 256, 256), preferred_element_type=jnp.float32
    )


def difference_kernel(
    rim, psf_rim, flags, canvas, above, below, science, science_above, science_below, bands,
    difference, padded, square, extended, packed, model,
):
    rows, cols = science.shape
    halo = above.shape[0]
    for k in range(extended.shape[0]):
        here = slice(k * LANES, (k + 1) * LANES)
        extended[k, :halo, :] = above[:, here].astype(jnp.float32)
        extended[k, halo : halo + rows, :] = canvas[:, here]
        extended[k, halo + rows : 2 * halo + rows, :] = below[:, here].astype(jnp.float32)
    pairs = model.shape[1] // 2
    pair_rows(extended, halo - rim - psf_rim, bands.shape[0], pairs, packed)
    total = jnp.zeros((rows, LANES), jnp.float32)
    body = slice(psf_rim, psf_rim + rows)
    bottom = slice(psf_rim + rows, 2 * psf_rim + rows)
    lane = lax.broadcasted_iota(jnp.int32, (padded.shape[1], LANES), 1)
    carried = jnp.zeros((padded.shape[1], LANES), jnp.float32)
    for k in range(cols // LANES):
        product = band_product(packed, bands, k)
        here = slice(k * LANES, (k + 1) * LANES)
        model[k, pl.ds(0, pairs, stride=2), :] = product[:, :LANES]
        model[k, pl.ds(1, pairs, stride=2), :] = product[:, LANES:]
        inner = science[:, here] - model[k, body, :]
        difference[:, here] = inner
        total = total + inner * inner
        top = jnp.where(flags[0, 0] > 0, science_above[:, here] - model[k, :psf_rim, :], 0.0)
        low = jnp.where(flags[0, 1] > 0, science_below[:, here] - model[k, bottom, :], 0.0)
        turned = pltpu.roll(jnp.concatenate([top, inner, low], axis=0), psf_rim, 1)
        padded[k, :, :] = jnp.where(lane < psf_rim, carried, turned)
        carried = turned
    padded[cols // LANES, :, :] = jnp.where(lane < psf_rim, carried, 0.0)
    square[...] = jnp.broadcast_to(jnp.sum(total), square.shape)


def response_kernel(padded, bands, response, packed, mixed):
    rows, cols = response.shape
    pairs = rows // 2
    pair_rows(padded, 0, bands.shape[0], pairs, packed)
    for k in range(cols // LANES):
        product = band_product(packed, bands, k)
        mixed[k, pl.ds(0, pairs, stride=2), :] = product[:, :LANES]
        mixed[k, pl.ds(1, pairs, stride=2), :] = product[:, LANES:]
        response[:, k * LANES : (k + 1) * LANES] = mixed[k]


def tap_rows(taps, width):
    reversed_taps = jnp.flip(taps[:, 1:], axis=1)
    gap = jnp.zeros((taps.shape[0], width - taps.shape[1]), jnp.float32)
    return jnp.concatenate([taps[:, :1], gap, reversed_taps], axis=1)


def shards(
    science,
    template,
    owner_map,
    covering,
    row_shift,
    col_shift,
    basis_cols,
    basis_rows,
    coeffs,
    psf_kernel,
):
    image_rows, image_cols = science.shape
    devices = lax.axis_size("visit")
    position = lax.axis_index("visit")
    held_piece = (position + 1) % devices
    visit_id = held_piece // PIECES
    piece_position = held_piece % PIECES
    slot_count = covering.shape[1]
    rim = basis_cols.shape[1] // 2
    psf_rim = psf_kernel.shape[0] // 2
    width = image_cols + LANES
    vmem = pl.BlockSpec(memory_space=pltpu.VMEM)
    smem = pl.BlockSpec(memory_space=pltpu.SMEM)

    pieces = gather_pieces(template, position)

    place = [(j + 1) % devices for j in range(devices)]
    down_pairs = [(i, (i + 1) % devices) for i in range(devices) if place[(i + 1) % devices] % PIECES]
    up_pairs = [((i + 1) % devices, i) for i in range(devices) if place[(i + 1) % devices] % PIECES]
    science_above = lax.ppermute(science[image_rows - psf_rim :], "visit", down_pairs)
    science_below = lax.ppermute(science[:psf_rim], "visit", up_pairs)

    matches = covering[0][:, None] == jnp.arange(devices, dtype=jnp.int32)[None, :]
    holders = jnp.sum(jnp.where(matches, owner_map[None, :], 0), axis=1)
    reach = len(BUFFER_OF[0]) // 2
    table = jnp.array(BUFFER_OF, jnp.int32)
    table_row = jnp.sum(jnp.where((jnp.arange(4) == position % 4)[:, None], table, 0), axis=0)
    chosen = (holders - position + reach)[:, None] == jnp.arange(2 * reach + 1)[None, :]
    buffers = jnp.sum(jnp.where(chosen, table_row[None, :], 0), axis=1)
    scalars = jnp.concatenate([jnp.zeros((1,), jnp.int32), buffers[1:], col_shift[0, 1:]])
    scalars = jnp.pad(scalars, (0, 16 - scalars.shape[0]))[None, :]
    flags = jnp.stack([piece_position != 0, piece_position != PIECES - 1]).astype(jnp.int32)[None, :]

    row_index = jnp.arange(image_rows, dtype=jnp.int32)
    source_row = row_index[None, :, None] - row_shift[0, 1:][:, None, None]
    rows_hot = (source_row == row_index[None, None, :]).astype(jnp.bfloat16)
    row_moved = row_index[None, :] - row_shift[0][:, None]
    padded_col = jnp.arange(width, dtype=jnp.int32) - rim
    col_moved = padded_col[None, :] - col_shift[0][:, None]
    row_inside = (row_moved >= 0) & (row_moved < image_rows)
    col_inside = (col_moved >= 0) & (col_moved < image_cols)
    coverage = jnp.zeros((image_rows, width), jnp.float32)
    for slot in range(slot_count):
        inside = row_inside[slot][:, None] & col_inside[slot][None, :]
        coverage = coverage + jnp.where(inside, 1.0, 0.0)
    in_image = (padded_col >= 0) & (padded_col < image_cols)
    recip = jnp.where(in_image[None, :], 1.0 / jnp.maximum(coverage, 1.0), 0.0)

    coeff_row = lax.dynamic_index_in_dim(coeffs, visit_id, 0, keepdims=False)
    weights = (coeff_row[:, None] * basis_rows).astype(jnp.bfloat16)
    model_taps = jnp.einsum(
        "bs,bt->st", weights, basis_cols.astype(jnp.bfloat16), preferred_element_type=jnp.float32
    )
    psf_taps = psf_kernel.astype(jnp.bfloat16).astype(jnp.float32)
    model_offsets = basis_rows.shape[1] + 1
    psf_offsets = psf_kernel.shape[0] + 1
    model_bands, psf_bands = pl.pallas_call(
        bands_kernel,
        out_shape=(
            jax.ShapeDtypeStruct((model_offsets, 256, 256), jnp.bfloat16),
            jax.ShapeDtypeStruct((psf_offsets, 256, 256), jnp.bfloat16),
        ),
        in_specs=[vmem, vmem],
        out_specs=(vmem, vmem),
    )(tap_rows(model_taps, 256), tap_rows(psf_taps, 256))

    canvas = pl.pallas_call(
        lambda *refs: canvas_kernel(rim, *refs),
        out_shape=jax.ShapeDtypeStruct((image_rows, width), jnp.float32),
        in_specs=[smem] + [vmem] * 9,
        out_specs=vmem,
        scratch_shapes=[pltpu.VMEM((image_rows, image_cols + 6 * LANES), jnp.float32)],
    )(scalars, rows_hot, recip, *pieces)

    halo = 16
    above = lax.ppermute(canvas[image_rows - halo :].astype(jnp.bfloat16), "visit", down_pairs)
    below = lax.ppermute(canvas[:halo].astype(jnp.bfloat16), "visit", up_pairs)

    pairs = 136
    difference, padded, square = pl.pallas_call(
        lambda *refs: difference_kernel(rim, psf_rim, *refs),
        out_shape=(
            jax.ShapeDtypeStruct((image_rows, image_cols), jnp.float32),
            jax.ShapeDtypeStruct((width // LANES, image_rows + 2 * psf_rim, LANES), jnp.float32),
            jax.ShapeDtypeStruct((8, LANES), jnp.float32),
        ),
        in_specs=[smem] + [vmem] * 7,
        out_specs=(vmem, vmem, vmem),
        scratch_shapes=[
            pltpu.VMEM((width // LANES, image_rows + 2 * halo + 8, LANES), jnp.float32),
            pltpu.VMEM((model_offsets, pairs, width), jnp.bfloat16),
            pltpu.VMEM((image_cols // LANES, 2 * pairs, LANES), jnp.float32),
        ],
    )(flags, canvas, above, below, science, science_above, science_below, model_bands)

    groups = [[(first + i - 1) % devices for i in range(PIECES)] for first in range(0, devices, PIECES)]
    total = square
    for turn in range(1, PIECES):
        links = [(g[i], g[(i + turn) % PIECES]) for g in groups for i in range(PIECES)]
        total = total + lax.ppermute(square, "visit", links)

    response = pl.pallas_call(
        response_kernel,
        out_shape=jax.ShapeDtypeStruct((image_rows, image_cols), jnp.float32),
        in_specs=[vmem, vmem],
        out_specs=vmem,
        scratch_shapes=[
            pltpu.VMEM((psf_offsets, image_rows // 2, width), jnp.bfloat16),
            pltpu.VMEM((image_cols // LANES, image_rows, LANES), jnp.float32),
        ],
    )(padded, psf_bands)
    variance = total[0, 0] / (PIECES * image_rows * image_cols)
    detection = response / jnp.sqrt(variance + 1e-06)
    return (difference, detection)


def solution(mesh):
    return jax.shard_map(
        shards,
        mesh=mesh,
        in_specs=(
            P(("groups", "visit"), None),
            P(("groups", "visit"), None),
            P("groups"),
            P(("groups", "visit"), None),
            P(("groups", "visit"), None),
            P(("groups", "visit"), None),
            P(),
            P(),
            P("groups", None),
            P(),
        ),
        out_specs=(P(("groups", "visit"), None), P(("groups", "visit"), None)),
        check_vma=False,
    )
```

```python
import jax
import jax.numpy as jnp
from jax import lax
from jax.experimental import pallas as pl
from jax.experimental.pallas import tpu as pltpu
from jax.sharding import PartitionSpec as P


PIECES = 4
LANES = 128

BUFFER_OF = ((4, 5, 6, 0, 1, 2, 3), (6, 5, 1, 0, 3, 2, 4), (4, 2, 3, 0, 1, 5, 6), (3, 2, 1, 0, 6, 5, 4))


def cost(megabytes):
    return pl.CostEstimate(flops=0, transcendentals=0, bytes_accessed=megabytes * 2**20)


def relay_kernel(far, pair, out):
    residue = lax.rem(lax.axis_index("visit"), 4)
    passes_far = (residue == 1) | (residue == 2)

    @pl.when(passes_far)
    def _():
        out[...] = far[...]

    @pl.when(jnp.logical_not(passes_far))
    def _():
        out[...] = pair[...]


def place_of():
    devices = lax.axis_size("visit")
    return lax.rem(lax.rem(lax.axis_index("visit") + 1, devices), PIECES)


def gather_pieces(own):
    count = lax.axis_size("visit")

    def move(value, pairs):
        kept = [(i, j) for i, j in pairs if 0 <= j < count]
        return lax.ppermute(value, "visit", kept)

    pair = move(own, [(i, i ^ 2) for i in range(count)])
    far = move(own, [(i, i + 3 if i % 2 else i - 3) for i in range(count)])
    partner = move(own, [(i, i ^ 1) for i in range(count)])
    whole = pl.BlockSpec(memory_space=pltpu.VMEM)
    relay = pl.pallas_call(
        relay_kernel,
        out_shape=jax.ShapeDtypeStruct(own.shape, own.dtype),
        in_specs=[whole, whole],
        out_specs=whole,
        compiler_params=pltpu.CompilerParams(vmem_limit_bytes=4 * 2**20),
        cost_estimate=cost(1),
        name="relay",
    )(far, pair)
    targets = {0: 4, 1: 1, 2: -1, 3: -4}
    relayed = move(relay, [(i, i + targets[i % 4]) for i in range(count)])
    crossed = move(pair, [(i, i ^ 1) for i in range(count)])
    relayed_crossed = move(relayed, [(i, i ^ 1) for i in range(count)])
    return (own, partner, pair, crossed, far, relayed, relayed_crossed)


CHUNK = 16


def spread(piece, turn, target, first):
    rows, cols = piece.shape
    blocks = cols // LANES

    def body(step, carry):
        row = pl.multiple_of(step * CHUNK, CHUNK)
        for k in range(blocks):
            tile = piece[pl.ds(row, CHUNK), k * LANES : (k + 1) * LANES].astype(jnp.float32)
            if turn is not None:
                tile = pltpu.roll(tile, turn, 1)
            target[pl.ds(first + row * blocks + k, CHUNK, stride=blocks), :] = tile
        return carry

    lax.fori_loop(0, rows // CHUNK, body, 0, unroll=4)


def shift_of(rows, blocks, row_shift, col_shift, valid):
    most = rows // 2
    base = (most + 1) * blocks
    lane = lax.broadcasted_iota(jnp.int32, (blocks, LANES), 1)
    block = lax.broadcasted_iota(jnp.int32, (blocks, LANES), 0)
    back = -col_shift
    start = lax.shift_right_arithmetic(back, 7)
    left = back - start * LANES
    turn = lax.bitwise_and(LANES - left, LANES - 1)
    limit = jnp.where(valid, blocks, -2 * blocks)
    here = block + start
    masks = (
        (lane < LANES - left) & (here >= 0) & (here < limit),
        (lane >= LANES - left) & (here >= -1) & (here < limit - 1),
    )
    return base, turn, base - row_shift * blocks + start, masks


def clear_ends(moved, rows, blocks):
    pad = rows // 2 * blocks
    base = pad + blocks
    moved[blocks:base, :] = jnp.zeros((pad, LANES), jnp.float32)
    moved[base + rows * blocks : base + rows * blocks + pad, :] = jnp.zeros((pad, LANES), jnp.float32)


def add_moved(rows, blocks, read, moves, write):
    def body(step, carry):
        for i in range(8):
            row = step * 8 + i
            value = read(row)
            for moved, start, masks in moves:
                low = moved[pl.ds(start + row * blocks, blocks), :]
                high = moved[pl.ds(start + row * blocks + 1, blocks), :]
                value = value + jnp.where(masks[0], low, jnp.where(masks[1], high, 0.0))
            write(row, value)
        return carry

    lax.fori_loop(0, rows // 8, body, 0, unroll=4)


def slot_of(covering, owner_map, slot):
    position = lax.axis_index("visit")
    residue = lax.rem(position, 4)
    distance = owner_map[covering[0, slot]] - position
    buffer = jnp.int32(0)
    for place, row in enumerate(BUFFER_OF):
        for index, held in enumerate(row):
            here = (residue == place) & (distance == index - len(row) // 2)
            buffer = jnp.where(here, held, buffer)
    return buffer


def late_slot(covering, owner_map, row_shift, col_shift, buffer):
    valid, rows, cols = jnp.int32(0), jnp.int32(0), jnp.int32(0)
    for slot in range(1, covering.shape[1]):
        here = slot_of(covering, owner_map, slot) == buffer
        valid = jnp.where(here, 1, valid)
        rows = jnp.where(here, row_shift[0, slot], rows)
        cols = jnp.where(here, col_shift[0, slot], cols)
    return valid > 0, rows, cols


def near_kernel(covering, owner_map, row_shift, col_shift, own_piece, *refs):
    pieces, (out, recip), (own, moved) = refs[:4], refs[4:6], refs[6:]
    rows, cols = own_piece.shape
    blocks = cols // LANES
    slots = moved.shape[0]
    spread(own_piece, None, own, 0)
    moves = []
    for slot in range(slots):
        held = slot_of(covering, owner_map, slot + 1)
        base, turn, start, masks = shift_of(
            rows, blocks, row_shift[0, slot + 1], col_shift[0, slot + 1], held <= len(pieces)
        )
        clear_ends(moved.at[slot], rows, blocks)
        for index in range(len(pieces)):

            @pl.when(held == index + 1)
            def _():
                spread(pieces[index], turn, moved.at[slot], base)

        moves.append((moved.at[slot], start, masks))

    def read(row):
        return own[pl.ds(pl.multiple_of(row * blocks, blocks), blocks), :]

    def write(row, value):
        out[row] = value

    add_moved(rows, blocks, read, moves, write)
    column = lax.broadcasted_iota(jnp.int32, (blocks, LANES), 0) * LANES
    column = column + lax.broadcasted_iota(jnp.int32, (blocks, LANES), 1)
    covers = []
    for slot in range(slots):
        source = column - col_shift[0, slot + 1]
        covers.append(jnp.where((source >= 0) & (source < cols), 1.0, 0.0))

    def cover(step, carry):
        for i in range(8):
            row = step * 8 + i
            total = jnp.ones((blocks, LANES), jnp.float32)
            for slot in range(slots):
                source = row - row_shift[0, slot + 1]
                inside = ((source >= 0) & (source < rows)).astype(jnp.float32)
                total = total + covers[slot] * inside
            recip[row] = 1.0 / total
        return carry

    lax.fori_loop(0, rows // 8, cover, 0, unroll=4)


def relayed_kernel(covering, owner_map, row_shift, col_shift, partial, piece, out, moved):
    rows, blocks, _ = partial.shape
    valid, row_move, col_move = late_slot(covering, owner_map, row_shift, col_shift, 5)
    base, turn, start, masks = shift_of(rows, blocks, row_move, col_move, valid)

    @pl.when(valid)
    def _():
        clear_ends(moved, rows, blocks)
        spread(piece, turn, moved, base)

    def write(row, value):
        out[row] = value

    add_moved(rows, blocks, lambda row: partial[row], [(moved, start, masks)], write)


def canvas_kernel(
    covering, owner_map, row_shift, col_shift, partial, piece, recip, first_rows, last_rows, out, to_inner, to_outer, moved,
):
    rows, blocks, _ = partial.shape
    valid, row_move, col_move = late_slot(covering, owner_map, row_shift, col_shift, 6)
    base, turn, start, masks = shift_of(rows, blocks, row_move, col_move, valid)

    @pl.when(valid)
    def _():
        clear_ends(moved, rows, blocks)
        spread(piece, turn, moved, base)

    def write(row, value):
        out[row] = value * recip[row]

    add_moved(rows, blocks, lambda row: partial[row], [(moved, start, masks)], write)
    edge = to_inner.shape[0] - first_rows.shape[0]
    even = lax.rem(place_of(), 2) == 0
    for message, up in ((to_inner, even), (to_outer, jnp.logical_not(even))):

        @pl.when(up)
        def _():
            message[:edge] = out[:edge].astype(jnp.bfloat16)
            message[edge:] = first_rows[...]

        @pl.when(jnp.logical_not(up))
        def _():
            message[:edge] = out[rows - edge :].astype(jnp.bfloat16)
            message[edge:] = last_rows[...]


def bands_of(taps, bands):
    count, lanes = taps.shape
    half = lanes // 2
    lower = lax.broadcasted_iota(jnp.int32, (lanes, lanes), 1) < half
    zero = jnp.zeros((lanes, lanes), jnp.float32)

    def table(tap, shift):
        if not 0 <= tap < count:
            return zero
        spread = jnp.broadcast_to(taps[tap : tap + 1, :], (lanes, lanes))
        return pltpu.roll(spread, shift, 1, stride=1, stride_axis=0)

    for offset in range(2 * bands.shape[1]):
        at = slice((offset % 2) * lanes, (offset % 2 + 1) * lanes)
        for pair in range(2):
            plain = table(offset - 2 * pair, 0)
            turned = table(offset - 2 * pair - 1, half)
            to = slice(pair * lanes, (pair + 1) * lanes)
            bands[0, offset // 2, at, to] = jnp.where(lower, plain, turned).astype(bands.dtype)
            bands[1, offset // 2, at, to] = jnp.where(lower, turned, plain).astype(bands.dtype)


def prepare_kernel(model_taps, psf_taps, top, bottom, model_bands, psf_bands, first_rows, last_rows, mixed):
    bands_of(model_taps, model_bands)
    bands_of(psf_taps, psf_bands)
    rows, cols = top.shape
    blocks = cols // LANES
    count = first_rows.shape[0] // 2
    for block, out, first in ((top, first_rows, 0), (bottom, last_rows, rows - count)):
        for k in range(blocks):
            mixed[pl.ds(k, rows, stride=blocks), :] = block[:, k * LANES : (k + 1) * LANES]
        for row in range(count):
            value = mixed[(first + row) * blocks : (first + row + 1) * blocks, :]
            high = value.astype(jnp.bfloat16)
            out[row] = high
            out[count + row] = (value - high.astype(jnp.float32)).astype(jnp.bfloat16)


def pack_rows(source, count, packed):
    blocks = 8
    lane = lax.broadcasted_iota(jnp.int32, (blocks, LANES), 1)
    block = lax.broadcasted_iota(jnp.int32, (blocks, LANES), 0)
    inner = block > 0
    outer = block < blocks - 1

    def sides(x):
        at = blocks * (x + 1)
        here = source[at : at + blocks, :]
        before = source[at - 1 : at - 1 + blocks, :]
        after = source[at + 1 : at + 1 + blocks, :]
        return (
            jnp.where(lane < 96, here, jnp.where(inner, before, 0.0)),
            jnp.where(lane >= 32, here, jnp.where(outer, after, 0.0)),
        )

    for phase in range(4):
        last = sides(phase)
        for h in range(1, count // 4):
            now = sides(4 * h + phase)
            odd, p = (h - 1) % 2, (h - 1) // 2
            for side in range(2):
                tile = jnp.concatenate([last[side], now[side]], axis=0).astype(jnp.bfloat16)
                to = slice((phase % 2) * LANES, (phase % 2 + 1) * LANES)
                packed[odd, side, phase // 2, 16 * p : 16 * p + 16, to] = tile
            last = now


def product_of(packed, bands, side, groups):
    chunks = bands.shape[1]
    left = []
    for chunk in range(chunks):
        q, pair = chunk // 2, chunk % 2
        first = 16 * (q // 2)
        left.append(packed[q % 2, side, pair, first : first + 8 * groups, :])
    right = bands[side].reshape(chunks * 256, 256)
    return jnp.dot(jnp.concatenate(left, axis=1), right, preferred_element_type=jnp.float32)


def unfold(packed, bands, groups, target):
    low = product_of(packed, bands, 0, groups)
    high = product_of(packed, bands, 1, groups)
    lower = lax.broadcasted_iota(jnp.int32, (8, LANES), 1) < LANES // 2
    for g in range(groups):
        rows = slice(8 * g, 8 * g + 8)
        for pair in range(2):
            lanes = slice(pair * LANES, (pair + 1) * LANES)
            a, b = low[rows, lanes], high[rows, lanes]
            to = 8 * (4 * g + 2 * pair)
            target[to : to + 8, :] = jnp.where(lower, a, b)
            target[to + 8 : to + 16, :] = pltpu.roll(jnp.where(lower, b, a), LANES // 2, 1)


def difference_kernel(
    rim, psf_rim, canvas, inner_rows, outer_rows, science, bands, difference, rounded, square, extended, packed, model,
):
    rows, cols = science.shape
    blocks = cols // LANES
    edge = rim + psf_rim
    first = blocks

    def put(x, values):
        extended[first + x * blocks : first + (x + values.shape[0]) * blocks, :] = values.reshape(-1, LANES)

    place = place_of()
    odd = lax.rem(place, 2) == 1
    put(edge, canvas[...])
    for swapped in range(2):

        @pl.when(odd == (swapped == 1))
        def _():
            above, below = (outer_rows, inner_rows) if swapped else (inner_rows, outer_rows)
            put(0, above[:edge].astype(jnp.float32))
            put(edge + rows, below[:edge].astype(jnp.float32))

    pack_rows(extended, rows + 2 * edge, packed)
    unfold(packed, bands, (rows + 2 * psf_rim) // 4, model)

    def body(step, total):
        row = pl.multiple_of(step * 8, 8)
        for k in range(blocks):
            here = slice(k * LANES, (k + 1) * LANES)
            at = pl.ds((row + psf_rim) * blocks + k, 8, stride=blocks)
            inner = science[pl.ds(row, 8), here] - model[at, :]
            difference[pl.ds(row, 8), here] = inner
            rounded[pl.ds(first + (row + psf_rim) * blocks + k, 8, stride=blocks), :] = inner
            total = total + inner * inner
        return total

    total = lax.fori_loop(0, rows // 8, body, jnp.zeros((8, LANES), jnp.float32), unroll=2)
    square[...] = jnp.broadcast_to(jnp.sum(total), square.shape)
    for swapped in range(2):

        @pl.when(odd == (swapped == 1))
        def _():
            above, below = (outer_rows, inner_rows) if swapped else (inner_rows, outer_rows)
            for joined, rows_of, x in ((place > 0, above, 0), (place < PIECES - 1, below, psf_rim + rows)):
                value = rows_of[edge : edge + psf_rim].astype(jnp.float32)
                value = value + rows_of[edge + psf_rim : edge + 2 * psf_rim].astype(jnp.float32)
                value = value.reshape(-1, LANES) - model[x * blocks : (x + psf_rim) * blocks, :]
                to = slice(first + x * blocks, first + (x + psf_rim) * blocks)
                rounded[to, :] = jnp.where(joined, value, 0.0)


def response_kernel(rounded, bands, response, packed, mixed):
    rows, cols = response.shape
    blocks = cols // LANES
    pack_rows(rounded, rounded.shape[0] // blocks - 2, packed)
    unfold(packed, bands, rows // 4, mixed)
    for row in range(0, rows, 8):
        for k in range(blocks):
            response[row : row + 8, k * LANES : (k + 1) * LANES] = mixed[pl.ds(row * blocks + k, 8, stride=blocks), :]


def detection_kernel(count, response, *refs):
    total = refs[0][...]
    for ref in refs[1:-1]:
        total = total + ref[...]
    scale = 1.0 / jnp.sqrt(total[:1, :1] / count + 1e-06)
    refs[-1][...] = response[...] * scale


def tap_rows(taps, width):
    rim = taps.shape[1] // 2
    turned = jnp.flip(taps, axis=1)
    gap = jnp.zeros((taps.shape[0], width - taps.shape[1]), jnp.float32)
    return jnp.concatenate([turned[:, rim:], gap, turned[:, :rim]], axis=1)


def shards(
    science,
    template,
    owner_map,
    covering,
    row_shift,
    col_shift,
    basis_cols,
    basis_rows,
    coeffs,
    psf_kernel,
):
    image_rows, image_cols = science.shape
    devices = lax.axis_size("visit")
    position = lax.axis_index("visit")
    held_piece = (position + 1) % devices
    visit_id = held_piece // PIECES
    slot_count = covering.shape[1]
    rim = basis_cols.shape[1] // 2
    psf_rim = psf_kernel.shape[0] // 2
    blocks = image_cols // LANES
    vmem = pl.BlockSpec(memory_space=pltpu.VMEM)
    smem = pl.BlockSpec(memory_space=pltpu.SMEM)

    pieces = gather_pieces(template)

    slot_args = (covering, owner_map, row_shift, col_shift)
    coeff_row = lax.dynamic_index_in_dim(coeffs, visit_id, 0, keepdims=False)
    weights = (coeff_row[:, None] * basis_rows).astype(jnp.bfloat16)
    model_taps = jnp.einsum(
        "bs,bt->st", weights, basis_cols.astype(jnp.bfloat16), preferred_element_type=jnp.float32
    )
    psf_taps = psf_kernel.astype(jnp.bfloat16).astype(jnp.float32)
    model_chunks = (basis_rows.shape[1] + 3) // 2
    psf_chunks = (psf_kernel.shape[0] + 3) // 2
    edge = rim + psf_rim
    sent = jax.ShapeDtypeStruct((edge + 2 * psf_rim, blocks, LANES), jnp.bfloat16)
    rim_rows = jax.ShapeDtypeStruct((2 * psf_rim, blocks, LANES), jnp.bfloat16)
    last_block = image_rows // 8 - 1
    model_bands, psf_bands, first_rows, last_rows = pl.pallas_call(
        prepare_kernel,
        out_shape=(
            jax.ShapeDtypeStruct((2, model_chunks, 256, 256), jnp.bfloat16),
            jax.ShapeDtypeStruct((2, psf_chunks, 256, 256), jnp.bfloat16),
            rim_rows,
            rim_rows,
        ),
        grid=(1,),
        in_specs=[
            vmem,
            vmem,
            pl.BlockSpec((8, image_cols), lambda i: (0, 0)),
            pl.BlockSpec((8, image_cols), lambda i: (last_block, 0)),
        ],
        out_specs=(vmem, vmem, vmem, vmem),
        scratch_shapes=[pltpu.VMEM((8 * blocks, LANES), jnp.float32)],
        compiler_params=pltpu.CompilerParams(vmem_limit_bytes=16 * 2**20),
        cost_estimate=cost(4),
        name="prepare",
    )(tap_rows(model_taps, LANES), tap_rows(psf_taps, LANES), science, science)

    moved_rows = (2 * image_rows + 3) * blocks
    canvas_shape = jax.ShapeDtypeStruct((image_rows, blocks, LANES), jnp.float32)
    moved = pltpu.VMEM((moved_rows, LANES), jnp.float32)
    partial, recip = pl.pallas_call(
        near_kernel,
        out_shape=(canvas_shape, canvas_shape),
        in_specs=[smem] * 4 + [vmem] * 5,
        out_specs=(vmem, vmem),
        scratch_shapes=[
            pltpu.VMEM((image_rows * blocks, LANES), jnp.float32),
            pltpu.VMEM((slot_count - 1, moved_rows, LANES), jnp.float32),
        ],
        compiler_params=pltpu.CompilerParams(vmem_limit_bytes=20 * 2**20),
        cost_estimate=cost(11),
        name="near",
    )(*slot_args, *pieces[:5])
    partial = pl.pallas_call(
        relayed_kernel,
        out_shape=canvas_shape,
        in_specs=[smem] * 4 + [vmem] * 2,
        out_specs=vmem,
        scratch_shapes=[moved],
        compiler_params=pltpu.CompilerParams(vmem_limit_bytes=12 * 2**20),
        cost_estimate=cost(5),
        name="relayed",
    )(*slot_args, partial, pieces[5])
    canvas, to_inner, to_outer = pl.pallas_call(
        canvas_kernel,
        out_shape=(canvas_shape, sent, sent),
        in_specs=[smem] * 4 + [vmem] * 5,
        out_specs=(vmem, vmem, vmem),
        scratch_shapes=[moved],
        compiler_params=pltpu.CompilerParams(vmem_limit_bytes=12 * 2**20),
        cost_estimate=cost(5),
        name="canvas",
    )(*slot_args, partial, pieces[6], recip, first_rows, last_rows)

    groups = [[(first + i - 1) % devices for i in range(PIECES)] for first in range(0, devices, PIECES)]

    def swap(value, pairs):
        return lax.ppermute(value, "visit", [(g[a], g[b]) for g in groups for a, b in pairs])

    inner_rows = swap(to_inner, [(1, 2), (2, 1)])
    outer_rows = swap(to_outer, [(0, 1), (1, 0), (2, 3), (3, 2)])

    rounded_rows = image_rows + 2 * psf_rim
    difference, rounded, square = pl.pallas_call(
        lambda *refs: difference_kernel(rim, psf_rim, *refs),
        out_shape=(
            jax.ShapeDtypeStruct((image_rows, image_cols), jnp.float32),
            jax.ShapeDtypeStruct(((rounded_rows + 2) * blocks, LANES), jnp.float32),
            jax.ShapeDtypeStruct((8, LANES), jnp.float32),
        ),
        in_specs=[vmem] * 5,
        out_specs=(vmem, vmem, vmem),
        scratch_shapes=[
            pltpu.VMEM(((image_rows + 2 * edge + 2) * blocks, LANES), jnp.float32),
            pltpu.VMEM((2, 2, 2, (image_rows + 2 * edge) // 8 * 16, 256), jnp.bfloat16),
            pltpu.VMEM((rounded_rows * blocks, LANES), jnp.float32),
        ],
        compiler_params=pltpu.CompilerParams(vmem_limit_bytes=20 * 2**20),
        cost_estimate=cost(14),
        name="difference",
    )(canvas, inner_rows, outer_rows, science, model_bands)

    totals = [square]
    for turn in (3, 1, 2):
        links = [(g[i], g[(i + turn) % PIECES]) for g in groups for i in range(PIECES)]
        totals.append(lax.ppermute(square, "visit", links))

    response = pl.pallas_call(
        response_kernel,
        out_shape=jax.ShapeDtypeStruct((image_rows, image_cols), jnp.float32),
        in_specs=[vmem, vmem],
        out_specs=vmem,
        scratch_shapes=[
            pltpu.VMEM((2, 2, 2, rounded_rows // 8 * 16, 256), jnp.bfloat16),
            pltpu.VMEM((image_rows * blocks, LANES), jnp.float32),
        ],
        compiler_params=pltpu.CompilerParams(vmem_limit_bytes=16 * 2**20),
        cost_estimate=cost(5),
        name="response",
    )(rounded, psf_bands)
    count = float(PIECES * image_rows * image_cols)
    detection = pl.pallas_call(
        lambda *refs: detection_kernel(count, *refs),
        out_shape=jax.ShapeDtypeStruct((image_rows, image_cols), jnp.float32),
        in_specs=[vmem] * (1 + PIECES),
        out_specs=vmem,
        compiler_params=pltpu.CompilerParams(vmem_limit_bytes=8 * 2**20),
        cost_estimate=cost(4),
        name="detection",
    )(response, *totals)
    return (difference, detection)


def solution(mesh):
    return jax.shard_map(
        shards,
        mesh=mesh,
        in_specs=(
            P(("groups", "visit"), None),
            P(("groups", "visit"), None),
            P("groups"),
            P(("groups", "visit"), None),
            P(("groups", "visit"), None),
            P(("groups", "visit"), None),
            P(),
            P(),
            P("groups", None),
            P(),
        ),
        out_specs=(P(("groups", "visit"), None), P(("groups", "visit"), None)),
        check_vma=False,
    )
```

```python
import jax
import jax.numpy as jnp
from jax import lax
from jax.experimental import pallas as pl
from jax.experimental.pallas import tpu as pltpu
from jax.sharding import PartitionSpec as P


PIECES = 4
SUMS = (((0, 2), (1, 3)), ((0, 1), (2, 3)), ((0, 3), (1, 2)))
LANES = 128

BUFFER_OF = ((4, 5, 6, 0, 1, 2, 3), (6, 5, 1, 0, 3, 2, 4), (4, 2, 3, 0, 1, 5, 6), (3, 2, 1, 0, 6, 5, 4))


def cost(megabytes):
    return pl.CostEstimate(flops=0, transcendentals=0, bytes_accessed=megabytes * 2**20)


def relay_kernel(far, pair, out):
    residue = lax.rem(lax.axis_index("visit"), 4)
    passes_far = (residue == 1) | (residue == 2)

    @pl.when(passes_far)
    def _():
        out[...] = far[...]

    @pl.when(jnp.logical_not(passes_far))
    def _():
        out[...] = pair[...]


def place_of():
    devices = lax.axis_size("visit")
    return lax.rem(lax.rem(lax.axis_index("visit") + 1, devices), PIECES)


def gather_pieces(own):
    count = lax.axis_size("visit")

    def move(value, pairs):
        kept = [(i, j) for i, j in pairs if 0 <= j < count]
        return lax.ppermute(value, "visit", kept)

    pair = move(own, [(i, i ^ 2) for i in range(count)])
    far = move(own, [(i, i + 3 if i % 2 else i - 3) for i in range(count)])
    partner = move(own, [(i, i ^ 1) for i in range(count)])
    whole = pl.BlockSpec(memory_space=pltpu.VMEM)
    relay = pl.pallas_call(
        relay_kernel,
        out_shape=jax.ShapeDtypeStruct(own.shape, own.dtype),
        in_specs=[whole, whole],
        out_specs=whole,
        compiler_params=pltpu.CompilerParams(vmem_limit_bytes=4 * 2**20),
        cost_estimate=cost(1),
        name="relay",
    )(far, pair)
    targets = {0: 4, 1: 1, 2: -1, 3: -4}
    relayed = move(relay, [(i, i + targets[i % 4]) for i in range(count)])
    crossed = move(pair, [(i, i ^ 1) for i in range(count)])
    relayed_crossed = move(relayed, [(i, i ^ 1) for i in range(count)])
    return (own, partner, pair, crossed, far, relayed, relayed_crossed)


CHUNK = 16
EDGE = 16


def spread(piece, turn, target, first):
    rows, cols = piece.shape
    blocks = cols // LANES

    def body(step, carry):
        row = pl.multiple_of(step * CHUNK, CHUNK)
        for k in range(blocks):
            tile = piece[pl.ds(row, CHUNK), k * LANES : (k + 1) * LANES].astype(jnp.float32)
            if turn is not None:
                tile = pltpu.roll(tile, turn, 1)
            target[pl.ds(first + row * blocks + k, CHUNK, stride=blocks), :] = tile
        return carry

    lax.fori_loop(0, rows // CHUNK, body, 0, unroll=4)


def shift_of(rows, blocks, row_shift, col_shift, valid):
    most = rows // 2
    base = (most + 1) * blocks
    lane = lax.broadcasted_iota(jnp.int32, (blocks, LANES), 1)
    block = lax.broadcasted_iota(jnp.int32, (blocks, LANES), 0)
    back = -col_shift
    start = lax.shift_right_arithmetic(back, 7)
    left = back - start * LANES
    turn = lax.bitwise_and(LANES - left, LANES - 1)
    limit = jnp.where(valid, blocks, -2 * blocks)
    here = block + start
    masks = (
        (lane < LANES - left) & (here >= 0) & (here < limit),
        (lane >= LANES - left) & (here >= -1) & (here < limit - 1),
    )
    return base, turn, base - row_shift * blocks + start, masks


def clear_ends(moved, rows, blocks):
    pad = rows // 2 * blocks
    base = pad + blocks
    moved[blocks:base, :] = jnp.zeros((pad, LANES), jnp.float32)
    moved[base + rows * blocks : base + rows * blocks + pad, :] = jnp.zeros((pad, LANES), jnp.float32)


def add_moved(rows, blocks, read, moves, write):
    def body(step, carry):
        for i in range(8):
            row = step * 8 + i
            value = read(row)
            for moved, start, masks in moves:
                low = moved[pl.ds(start + row * blocks, blocks), :]
                high = moved[pl.ds(start + row * blocks + 1, blocks), :]
                value = value + jnp.where(masks[0], low, jnp.where(masks[1], high, 0.0))
            write(row, value)
        return carry

    lax.fori_loop(0, rows // 8, body, 0, unroll=4)


def slot_of(covering, owner_map, slot):
    position = lax.axis_index("visit")
    residue = lax.rem(position, 4)
    distance = owner_map[covering[0, slot]] - position
    buffer = jnp.int32(0)
    for place, row in enumerate(BUFFER_OF):
        for index, held in enumerate(row):
            here = (residue == place) & (distance == index - len(row) // 2)
            buffer = jnp.where(here, held, buffer)
    return buffer


def near_kernel(table, own, *refs):
    pieces, (out, recip, moved) = refs[:4], refs[4:]
    rows, cols = pieces[0].shape
    blocks = cols // LANES
    slots = moved.shape[0]
    moves = []
    for slot in range(slots):
        held = table[0, slot]
        base, turn, start, masks = shift_of(
            rows, blocks, table[0, slots + slot], table[0, 2 * slots + slot], held <= len(pieces)
        )
        clear_ends(moved.at[slot], rows, blocks)
        for index in range(len(pieces)):

            @pl.when(held == index + 1)
            def _():
                spread(pieces[index], turn, moved.at[slot], base)

        moves.append((moved.at[slot], start, masks))

    def read(row):
        return own[pl.ds(pl.multiple_of(row * blocks, blocks), blocks), :]

    def write(row, value):
        out[row] = value

    add_moved(rows, blocks, read, moves, write)
    column = lax.broadcasted_iota(jnp.int32, (blocks, LANES), 0) * LANES
    column = column + lax.broadcasted_iota(jnp.int32, (blocks, LANES), 1)
    covers = []
    for slot in range(slots):
        source = column - table[0, 2 * slots + slot]
        covers.append(jnp.where((source >= 0) & (source < cols), 1.0, 0.0))

    def cover(step, carry):
        for i in range(8):
            row = step * 8 + i
            total = jnp.ones((blocks, LANES), jnp.float32)
            for slot in range(slots):
                source = row - table[0, slots + slot]
                inside = ((source >= 0) & (source < rows)).astype(jnp.float32)
                total = total + covers[slot] * inside
            recip[row] = 1.0 / total
        return carry

    lax.fori_loop(0, rows // 8, cover, 0, unroll=4)


def relayed_kernel(table, partial, piece, out, moved):
    rows, blocks, _ = partial.shape
    first = table.shape[1] - 6
    valid = table[0, first] > 0
    base, turn, start, masks = shift_of(rows, blocks, table[0, first + 1], table[0, first + 2], valid)

    @pl.when(valid)
    def _():
        clear_ends(moved, rows, blocks)
        spread(piece, turn, moved, base)

    def write(row, value):
        out[row] = value

    add_moved(rows, blocks, lambda row: partial[row], [(moved, start, masks)], write)


def canvas_kernel(
    table, partial, piece, recip, first_rows, last_rows, out, to_inner, to_outer, moved,
):
    rows, blocks, _ = partial.shape
    first = table.shape[1] - 3
    valid = table[0, first] > 0
    base, turn, start, masks = shift_of(rows, blocks, table[0, first + 1], table[0, first + 2], valid)

    @pl.when(valid)
    def _():
        clear_ends(moved, rows, blocks)
        spread(piece, turn, moved, base)

    def write(row, value):
        out[pl.ds(pl.multiple_of(row * blocks, blocks), blocks), :] = value * recip[row]

    add_moved(rows, blocks, lambda row: partial[row], [(moved, start, masks)], write)

    def rows_of(first, count):
        return out[first * blocks : (first + count) * blocks, :].reshape(count, blocks, LANES).astype(jnp.bfloat16)

    edge = to_inner.shape[0] - first_rows.shape[0]
    even = lax.rem(place_of(), 2) == 0
    for message, up in ((to_inner, even), (to_outer, jnp.logical_not(even))):

        @pl.when(up)
        def _():
            message[:edge] = rows_of(0, edge)
            message[edge:] = first_rows[...]

        @pl.when(jnp.logical_not(up))
        def _():
            message[:edge] = rows_of(rows - edge, edge)
            message[edge:] = last_rows[...]


def bands_of(taps, bands):
    count, lanes = taps.shape
    half = lanes // 2
    lower = lax.broadcasted_iota(jnp.int32, (lanes, lanes), 1) < half
    zero = jnp.zeros((lanes, lanes), jnp.float32)

    def table(tap, shift):
        if not 0 <= tap < count:
            return zero
        spread = jnp.broadcast_to(taps[tap : tap + 1, :], (lanes, lanes))
        return pltpu.roll(spread, shift, 1, stride=1, stride_axis=0)

    for offset in range(2 * bands.shape[1]):
        at = slice((offset % 2) * lanes, (offset % 2 + 1) * lanes)
        for pair in range(2):
            plain = table(offset - 2 * pair, 0)
            turned = table(offset - 2 * pair - 1, half)
            to = slice(pair * lanes, (pair + 1) * lanes)
            bands[0, offset // 2, at, to] = jnp.where(lower, plain, turned).astype(bands.dtype)
            bands[1, offset // 2, at, to] = jnp.where(lower, turned, plain).astype(bands.dtype)


def prepare_kernel(
    covering_in, owner_in, row_in, col_in, model_taps, psf_taps, science_in, piece_in,
    table, model_bands, psf_bands, first_rows, last_rows, turned, own,
    covering, owner_map, row_shift, col_shift, science, piece, arrived,
):
    sources = (covering_in, owner_in, row_in, col_in, science_in, piece_in)
    copies = [
        pltpu.make_async_copy(source, target, arrived.at[index])
        for index, (source, target) in enumerate(
            zip(sources, (covering, owner_map, row_shift, col_shift, science, piece))
        )
    ]
    for copy in copies:
        copy.start()
    bands_of(model_taps, model_bands)
    bands_of(psf_taps, psf_bands)
    for copy in copies:
        copy.wait()
    slots = covering.shape[1] - 1
    late = [[jnp.int32(0)] * 3 for _ in range(2)]
    for slot in range(slots):
        held = slot_of(covering, owner_map, slot + 1)
        entry = (held, row_shift[0, slot + 1], col_shift[0, slot + 1])
        for index in range(3):
            table[0, index * slots + slot] = entry[index]
        for buffer in range(2):
            here = held == 5 + buffer
            values = (jnp.int32(1), entry[1], entry[2])
            late[buffer] = [jnp.where(here, new, old) for new, old in zip(values, late[buffer])]
    for buffer in range(2):
        for index in range(3):
            table[0, 3 * (slots + buffer) + index] = late[buffer][index]
    spread(piece, None, own, 0)
    rows, cols = science.shape
    blocks = cols // LANES
    for row in range(0, rows, CHUNK):
        for k in range(blocks):
            at = pl.ds(row * blocks + k, CHUNK, stride=blocks)
            turned[at, :] = science[row : row + CHUNK, k * LANES : (k + 1) * LANES]
    count = first_rows.shape[0] // 2
    for out, first in ((first_rows, 0), (last_rows, rows - count)):
        for row in range(count):
            value = turned[(first + row) * blocks : (first + row + 1) * blocks, :]
            high = value.astype(jnp.bfloat16)
            out[row] = high
            out[count + row] = (value - high.astype(jnp.float32)).astype(jnp.bfloat16)


def pack_rows(source, start, steps, packed, base):
    blocks = 8
    lane = lax.broadcasted_iota(jnp.int32, (blocks, LANES), 1)
    block = lax.broadcasted_iota(jnp.int32, (blocks, LANES), 0)
    inner = block > 0
    outer = block < blocks - 1

    def sides(x):
        at = start + blocks * x
        here = source[at : at + blocks, :]
        before = source[at - 1 : at - 1 + blocks, :]
        after = source[at + 1 : at + 1 + blocks, :]
        return (
            jnp.where(lane < 96, here, jnp.where(inner, before, 0.0)),
            jnp.where(lane >= 32, here, jnp.where(outer, after, 0.0)),
        )

    for phase in range(4):
        last = sides(phase)
        for h in range(1, steps):
            now = sides(4 * h + phase)
            odd, p = (h - 1) % 2, base + (h - 1) // 2
            for side in range(2):
                tile = jnp.concatenate([last[side], now[side]], axis=0).astype(jnp.bfloat16)
                to = slice((phase % 2) * LANES, (phase % 2 + 1) * LANES)
                packed[odd, side, phase // 2, 16 * p : 16 * p + 16, to] = tile
            last = now


def product_of(packed, bands, side, parts):
    chunks = bands.shape[1]
    left = []
    for chunk in range(chunks):
        q, pair = chunk // 2, chunk % 2
        rows = []
        for base, groups in parts:
            first = 16 * (base + q // 2)
            rows.append(packed[q % 2, side, pair, first : first + 8 * groups, :])
        left.append(rows[0] if len(rows) == 1 else jnp.concatenate(rows, axis=0))
    right = bands[side].reshape(chunks * 256, 256)
    return jnp.dot(jnp.concatenate(left, axis=1), right, preferred_element_type=jnp.float32)


def unfold(packed, bands, parts, put):
    low = product_of(packed, bands, 0, parts)
    high = product_of(packed, bands, 1, parts)
    lower = lax.broadcasted_iota(jnp.int32, (8, LANES), 1) < LANES // 2
    for g in range(sum(groups for _, groups in parts)):
        rows = slice(8 * g, 8 * g + 8)
        for pair in range(2):
            lanes = slice(pair * LANES, (pair + 1) * LANES)
            a, b = low[rows, lanes], high[rows, lanes]
            put(4 * g + 2 * pair, jnp.where(lower, a, b))
            put(4 * g + 2 * pair + 1, pltpu.roll(jnp.where(lower, b, a), LANES // 2, 1))


def interior_kernel(
    rim, psf_rim, canvas, science, model_bands, psf_bands, difference, response, square, packed, packed_psf,
):
    blocks = 8
    rows = canvas.shape[0] // blocks
    first = EDGE - psf_rim
    groups = (rows - 2 * first) // 4
    pack_rows(canvas, (first - rim) * blocks, groups + model_bands.shape[1] // 2 - 1, packed, 0)
    totals = [jnp.zeros((blocks, LANES), jnp.float32) for _ in range(4)]

    def put(i, value):
        at = slice((first + i) * blocks, (first + i + 1) * blocks)
        value = science[at, :] - value
        difference[at, :] = value
        totals[i % 4] = totals[i % 4] + value * value

    unfold(packed, model_bands, [(0, groups)], put)
    square[...] = (totals[0] + totals[1]) + (totals[2] + totals[3])
    groups = (rows - 2 * EDGE) // 4
    pack_rows(difference, first * blocks, groups + psf_bands.shape[1] // 2 - 1, packed_psf, 0)

    def put_response(i, value):
        response[(EDGE + i) * blocks : (EDGE + i + 1) * blocks, :] = value

    unfold(packed_psf, psf_bands, [(0, groups)], put_response)


def edge_kernel(
    rim, psf_rim, canvas, inner_rows, outer_rows, science, bands, partial, top, bottom, square, joint, packed,
):
    blocks = 8
    rows = canvas.shape[0] // blocks
    edge = rim + psf_rim
    groups = EDGE // 4
    span = EDGE + 2 * rim
    starts = (blocks, (span + 3) * blocks)
    place = place_of()
    odd = lax.rem(place, 2) == 1
    own = span - edge
    joint[starts[0] + edge * blocks : starts[0] + span * blocks, :] = canvas[: own * blocks, :]
    joint[starts[1] : starts[1] + own * blocks, :] = canvas[(rows - own) * blocks :, :]
    for swapped in range(2):

        @pl.when(odd == (swapped == 1))
        def _():
            above, below = (outer_rows, inner_rows) if swapped else (inner_rows, outer_rows)
            to = starts[0]
            joint[to : to + edge * blocks, :] = above[:edge].astype(jnp.float32).reshape(-1, LANES)
            to = starts[1] + own * blocks
            joint[to : to + edge * blocks, :] = below[:edge].astype(jnp.float32).reshape(-1, LANES)
            for source, at in ((above, 0), (below, psf_rim)):
                value = source[edge : edge + psf_rim].astype(jnp.float32)
                value = value + source[edge + psf_rim : edge + 2 * psf_rim].astype(jnp.float32)
                to = (2 * (span + 3) + at) * blocks
                joint[to : to + psf_rim * blocks, :] = value.reshape(-1, LANES)

    steps = groups + bands.shape[1] // 2 - 1
    pairs = steps // 2
    pack_rows(joint, starts[0], steps, packed, 0)
    pack_rows(joint, starts[1], steps, packed, pairs)
    totals = [partial[...], jnp.zeros((blocks, LANES), jnp.float32)]

    def put(i, value):
        side, row = i // EDGE, i % EDGE
        target = (top, bottom)[side]
        at = slice(row * blocks, (row + 1) * blocks)
        outside = row < psf_rim if side == 0 else row >= EDGE - psf_rim
        if outside:
            which = row if side == 0 else psf_rim + row - (EDGE - psf_rim)
            to = (2 * (span + 3) + which) * blocks
            joined = place > 0 if side == 0 else place < PIECES - 1
            target[at, :] = jnp.where(joined, joint[to : to + blocks, :] - value, 0.0)
        else:
            to = (row - psf_rim if side == 0 else rows - EDGE + psf_rim + row) * blocks
            value = science[to : to + blocks, :] - value
            target[at, :] = value
            totals[side] = totals[side] + value * value

    unfold(packed, bands, [(0, groups), (pairs, groups)], put)
    square[...] = jnp.broadcast_to(jnp.sum(totals[0] + totals[1]), square.shape)


def rest_kernel(psf_rim, top, bottom, inside, bands, difference, response, joint, packed):
    blocks = 8
    rows, _ = difference.shape
    groups = EDGE // 4
    span = EDGE + 2 * psf_rim
    more = span - EDGE
    starts = (blocks, (span + 3) * blocks)
    joint[starts[0] : starts[0] + EDGE * blocks, :] = top[...]
    from_row = EDGE - psf_rim
    to = starts[0] + EDGE * blocks
    joint[to : to + more * blocks, :] = inside[from_row * blocks : (from_row + more) * blocks, :]
    from_row = rows - EDGE + psf_rim - more
    joint[starts[1] : starts[1] + more * blocks, :] = inside[from_row * blocks : (from_row + more) * blocks, :]
    joint[starts[1] + more * blocks : starts[1] + span * blocks, :] = bottom[...]
    steps = groups + bands.shape[1] // 2 - 1
    pairs = (steps + 1) // 2
    pack_rows(joint, starts[0], steps, packed, 0)
    pack_rows(joint, starts[1], steps, packed, pairs)

    def put(i, value):
        response[i * blocks : (i + 1) * blocks, :] = value

    unfold(packed, bands, [(0, groups), (pairs, groups)], put)
    for row in range(0, rows, 8):
        if row < EDGE:
            source, at = joint, starts[0] + (row + psf_rim) * blocks
        elif row >= rows - EDGE:
            source, at = joint, starts[1] + (row - (rows - EDGE - psf_rim)) * blocks
        else:
            source, at = inside, row * blocks
        for k in range(blocks):
            difference[row : row + 8, k * LANES : (k + 1) * LANES] = source[pl.ds(at + k, 8, stride=blocks), :]


def detection_kernel(count, inside, ends, *refs):
    out = refs[-1]
    total = refs[0][...]
    for ref in refs[1:-1]:
        total = total + ref[...]
    scale = 1.0 / jnp.sqrt(total / count + 1e-06)
    rows, cols = out.shape
    blocks = cols // LANES
    for row in range(0, rows, 8):
        if row < EDGE:
            source, at = ends, row * blocks
        elif row >= rows - EDGE:
            source, at = ends, (row - (rows - 2 * EDGE)) * blocks
        else:
            source, at = inside, row * blocks
        for k in range(blocks):
            out[row : row + 8, k * LANES : (k + 1) * LANES] = source[pl.ds(at + k, 8, stride=blocks), :] * scale


def tap_rows(taps, width):
    rim = taps.shape[1] // 2
    turned = jnp.flip(taps, axis=1)
    gap = jnp.zeros((taps.shape[0], width - taps.shape[1]), jnp.float32)
    return jnp.concatenate([turned[:, rim:], gap, turned[:, :rim]], axis=1)


def shards(
    science,
    template,
    owner_map,
    covering,
    row_shift,
    col_shift,
    basis_cols,
    basis_rows,
    coeffs,
    psf_kernel,
):
    image_rows, image_cols = science.shape
    devices = lax.axis_size("visit")
    position = lax.axis_index("visit")
    held_piece = (position + 1) % devices
    visit_id = held_piece // PIECES
    slot_count = covering.shape[1]
    rim = basis_cols.shape[1] // 2
    psf_rim = psf_kernel.shape[0] // 2
    blocks = image_cols // LANES
    vmem = pl.BlockSpec(memory_space=pltpu.VMEM)
    smem = pl.BlockSpec(memory_space=pltpu.SMEM)
    in_hbm = pl.BlockSpec(memory_space=pltpu.HBM)

    pieces = gather_pieces(template)

    coeff_row = lax.dynamic_index_in_dim(coeffs, visit_id, 0, keepdims=False)
    weights = (coeff_row[:, None] * basis_rows).astype(jnp.bfloat16)
    model_taps = jnp.einsum(
        "bs,bt->st", weights, basis_cols.astype(jnp.bfloat16), preferred_element_type=jnp.float32
    )
    psf_taps = psf_kernel.astype(jnp.bfloat16).astype(jnp.float32)
    model_chunks = (basis_rows.shape[1] + 3) // 2
    psf_chunks = (psf_kernel.shape[0] + 3) // 2
    edge = rim + psf_rim
    sent = jax.ShapeDtypeStruct((edge + 2 * psf_rim, blocks, LANES), jnp.bfloat16)
    rim_rows = jax.ShapeDtypeStruct((2 * psf_rim, blocks, LANES), jnp.bfloat16)
    turned_shape = jax.ShapeDtypeStruct((image_rows * blocks, LANES), jnp.float32)
    table, model_bands, psf_bands, first_rows, last_rows, turned, own = pl.pallas_call(
        prepare_kernel,
        out_shape=(
            jax.ShapeDtypeStruct((1, 3 * (slot_count + 1)), jnp.int32),
            jax.ShapeDtypeStruct((2, model_chunks, 256, 256), jnp.bfloat16),
            jax.ShapeDtypeStruct((2, psf_chunks, 256, 256), jnp.bfloat16),
            rim_rows,
            rim_rows,
            turned_shape,
            turned_shape,
        ),
        in_specs=[in_hbm] * 4 + [vmem] * 2 + [in_hbm] * 2,
        out_specs=(smem,) + (vmem,) * 6,
        scratch_shapes=[
            pltpu.SMEM(covering.shape, jnp.int32),
            pltpu.SMEM(owner_map.shape, jnp.int32),
            pltpu.SMEM(row_shift.shape, jnp.int32),
            pltpu.SMEM(col_shift.shape, jnp.int32),
            pltpu.VMEM(science.shape, science.dtype),
            pltpu.VMEM(template.shape, template.dtype),
            pltpu.SemaphoreType.DMA((6,)),
        ],
        compiler_params=pltpu.CompilerParams(vmem_limit_bytes=16 * 2**20),
        cost_estimate=cost(4),
        name="prepare",
    )(
        covering, owner_map, row_shift, col_shift,
        tap_rows(model_taps, LANES), tap_rows(psf_taps, LANES), science, template,
    )

    moved_rows = (2 * image_rows + 3) * blocks
    canvas_shape = jax.ShapeDtypeStruct((image_rows, blocks, LANES), jnp.float32)
    moved = pltpu.VMEM((moved_rows, LANES), jnp.float32)
    partial, recip = pl.pallas_call(
        near_kernel,
        out_shape=(canvas_shape, canvas_shape),
        in_specs=[smem] + [vmem] * 5,
        out_specs=(vmem, vmem),
        scratch_shapes=[
            pltpu.VMEM((slot_count - 1, moved_rows, LANES), jnp.float32),
        ],
        compiler_params=pltpu.CompilerParams(vmem_limit_bytes=20 * 2**20),
        cost_estimate=cost(11),
        name="near",
    )(table, own, *pieces[1:5])
    partial = pl.pallas_call(
        relayed_kernel,
        out_shape=canvas_shape,
        in_specs=[smem] + [vmem] * 2,
        out_specs=vmem,
        scratch_shapes=[moved],
        compiler_params=pltpu.CompilerParams(vmem_limit_bytes=12 * 2**20),
        cost_estimate=cost(5),
        name="relayed",
    )(table, partial, pieces[5])
    canvas, to_inner, to_outer = pl.pallas_call(
        canvas_kernel,
        out_shape=(turned_shape, sent, sent),
        in_specs=[smem] + [vmem] * 5,
        out_specs=(vmem, vmem, vmem),
        scratch_shapes=[moved],
        compiler_params=pltpu.CompilerParams(vmem_limit_bytes=12 * 2**20),
        cost_estimate=cost(5),
        name="canvas",
    )(table, partial, pieces[6], recip, first_rows, last_rows)

    groups = [[(first + i - 1) % devices for i in range(PIECES)] for first in range(0, devices, PIECES)]

    def swap(value, pairs):
        return lax.ppermute(value, "visit", [(g[a], g[b]) for g in groups for a, b in pairs])

    inner_rows = swap(to_inner, [(1, 2), (2, 1)])
    outer_rows = swap(to_outer, [(0, 1), (1, 0), (2, 3), (3, 2)])

    square_shape = jax.ShapeDtypeStruct((8, LANES), jnp.float32)
    inside, inside_response, inside_square = pl.pallas_call(
        lambda *refs: interior_kernel(rim, psf_rim, *refs),
        out_shape=(turned_shape, turned_shape, square_shape),
        in_specs=[vmem] * 4,
        out_specs=(vmem, vmem, vmem),
        scratch_shapes=[
            pltpu.VMEM((2, 2, 2, (image_rows // 8 + 2) * 16, 256), jnp.bfloat16),
            pltpu.VMEM((2, 2, 2, (image_rows // 8 + 2) * 16, 256), jnp.bfloat16),
        ],
        compiler_params=pltpu.CompilerParams(vmem_limit_bytes=20 * 2**20),
        cost_estimate=cost(12),
        name="interior",
    )(canvas, turned, model_bands, psf_bands)
    end_shape = jax.ShapeDtypeStruct((EDGE * blocks, LANES), jnp.float32)
    top, bottom, square = pl.pallas_call(
        lambda *refs: edge_kernel(rim, psf_rim, *refs),
        out_shape=(end_shape, end_shape, square_shape),
        in_specs=[vmem] * 6,
        out_specs=(vmem, vmem, vmem),
        scratch_shapes=[
            pltpu.VMEM(((2 * (EDGE + 2 * rim + 3) + 2 * psf_rim) * blocks, LANES), jnp.float32),
            pltpu.VMEM((2, 2, 2, (EDGE // 4 + model_chunks) * 16, 256), jnp.bfloat16),
        ],
        compiler_params=pltpu.CompilerParams(vmem_limit_bytes=16 * 2**20),
        cost_estimate=cost(4),
        name="edge",
    )(canvas, inner_rows, outer_rows, turned, model_bands, inside_square)

    totals = [square]
    for turn in SUMS:
        if isinstance(turn, int):
            links = [(g[i], g[(i + turn) % PIECES]) for g in groups for i in range(PIECES)]
        else:
            links = [(g[a], g[b]) for g in groups for p in turn for a, b in (p, p[::-1])]
        totals.append(lax.ppermute(square, "visit", links))

    difference, ends = pl.pallas_call(
        lambda *refs: rest_kernel(psf_rim, *refs),
        out_shape=(
            jax.ShapeDtypeStruct((image_rows, image_cols), jnp.float32),
            jax.ShapeDtypeStruct((2 * EDGE * blocks, LANES), jnp.float32),
        ),
        in_specs=[vmem] * 4,
        out_specs=(vmem, vmem),
        scratch_shapes=[
            pltpu.VMEM((2 * (EDGE + 2 * psf_rim + 3) * blocks, LANES), jnp.float32),
            pltpu.VMEM((2, 2, 2, (EDGE // 4 + psf_chunks) * 16, 256), jnp.bfloat16),
        ],
        compiler_params=pltpu.CompilerParams(vmem_limit_bytes=12 * 2**20),
        cost_estimate=cost(5),
        name="rest",
    )(top, bottom, inside, psf_bands)
    count = float(PIECES * image_rows * image_cols)
    detection = pl.pallas_call(
        lambda *refs: detection_kernel(count, *refs),
        out_shape=jax.ShapeDtypeStruct((image_rows, image_cols), jnp.float32),
        in_specs=[vmem] * (2 + PIECES),
        out_specs=vmem,
        compiler_params=pltpu.CompilerParams(vmem_limit_bytes=8 * 2**20),
        cost_estimate=cost(4),
        name="detection",
    )(inside_response, ends, *totals)
    return (difference, detection)


def solution(mesh):
    return jax.shard_map(
        shards,
        mesh=mesh,
        in_specs=(
            P(("groups", "visit"), None),
            P(("groups", "visit"), None),
            P("groups"),
            P(("groups", "visit"), None),
            P(("groups", "visit"), None),
            P(("groups", "visit"), None),
            P(),
            P(),
            P("groups", None),
            P(),
        ),
        out_specs=(P(("groups", "visit"), None), P(("groups", "visit"), None)),
        check_vma=False,
    )
```

```python
import jax
import jax.numpy as jnp
from jax import lax
from jax.experimental import pallas as pl
from jax.experimental.pallas import tpu as pltpu
from jax.sharding import PartitionSpec as P


PIECES = 4
SUMS = (((0, 2), (1, 3)), ((0, 1), (2, 3)), ((0, 3), (1, 2)))
LANES = 128

BUFFER_OF = ((4, 5, 6, 0, 1, 2, 3), (6, 5, 1, 0, 3, 2, 4), (4, 2, 3, 0, 1, 5, 6), (3, 2, 1, 0, 6, 5, 4))


def cost(megabytes):
    return pl.CostEstimate(flops=0, transcendentals=0, bytes_accessed=megabytes * 2**20)


def relay_kernel(far, pair, out):
    residue = lax.rem(lax.axis_index("visit"), 4)
    passes_far = (residue == 1) | (residue == 2)

    @pl.when(passes_far)
    def _():
        out[...] = far[...]

    @pl.when(jnp.logical_not(passes_far))
    def _():
        out[...] = pair[...]


def place_of():
    devices = lax.axis_size("visit")
    return lax.rem(lax.rem(lax.axis_index("visit") + 1, devices), PIECES)


def gather_pieces(own):
    count = lax.axis_size("visit")

    def move(value, pairs):
        kept = [(i, j) for i, j in pairs if 0 <= j < count]
        return lax.ppermute(value, "visit", kept)

    pair = move(own, [(i, i ^ 2) for i in range(count)])
    far = move(own, [(i, i + 3 if i % 2 else i - 3) for i in range(count)])
    partner = move(own, [(i, i ^ 1) for i in range(count)])
    whole = pl.BlockSpec(memory_space=pltpu.VMEM)
    relay = pl.pallas_call(
        relay_kernel,
        out_shape=jax.ShapeDtypeStruct(own.shape, own.dtype),
        in_specs=[whole, whole],
        out_specs=whole,
        compiler_params=pltpu.CompilerParams(vmem_limit_bytes=4 * 2**20),
        cost_estimate=cost(1),
        name="relay",
    )(far, pair)
    targets = {0: 4, 1: 1, 2: -1, 3: -4}
    relayed = move(relay, [(i, i + targets[i % 4]) for i in range(count)])
    crossed = move(pair, [(i, i ^ 1) for i in range(count)])
    relayed_crossed = move(relayed, [(i, i ^ 1) for i in range(count)])
    return (own, partner, pair, crossed, far, relayed, relayed_crossed)


CHUNK = 16
EDGE = 16
STEPS = 2


def spread(piece, turn, target, first):
    rows, cols = piece.shape
    blocks = cols // LANES

    def body(step, carry):
        row = pl.multiple_of(step * CHUNK, CHUNK)
        for k in range(blocks):
            tile = piece[pl.ds(row, CHUNK), k * LANES : (k + 1) * LANES].astype(jnp.float32)
            if turn is not None:
                tile = pltpu.roll(tile, turn, 1)
            target[pl.ds(first + row * blocks + k, CHUNK, stride=blocks), :] = tile
        return carry

    lax.fori_loop(0, rows // CHUNK, body, 0, unroll=4)


def shift_of(rows, blocks, row_shift, col_shift, valid):
    most = rows // 2
    base = (most + 1) * blocks
    lane = lax.broadcasted_iota(jnp.int32, (blocks, LANES), 1)
    block = lax.broadcasted_iota(jnp.int32, (blocks, LANES), 0)
    back = -col_shift
    start = lax.shift_right_arithmetic(back, 7)
    left = back - start * LANES
    turn = lax.bitwise_and(LANES - left, LANES - 1)
    limit = jnp.where(valid, blocks, -2 * blocks)
    here = block + start
    masks = (
        (lane < LANES - left) & (here >= 0) & (here < limit),
        (lane >= LANES - left) & (here >= -1) & (here < limit - 1),
    )
    return base, turn, base - row_shift * blocks + start, masks


def clear_ends(moved, rows, blocks):
    pad = rows // 2 * blocks
    base = pad + blocks
    moved[blocks:base, :] = jnp.zeros((pad, LANES), jnp.float32)
    moved[base + rows * blocks : base + rows * blocks + pad, :] = jnp.zeros((pad, LANES), jnp.float32)


def add_moved(rows, blocks, read, moves, write):
    def body(step, carry):
        for i in range(8):
            row = step * 8 + i
            value = read(row)
            for moved, start, masks in moves:
                low = moved[pl.ds(start + row * blocks, blocks), :]
                high = moved[pl.ds(start + row * blocks + 1, blocks), :]
                value = value + jnp.where(masks[0], low, jnp.where(masks[1], high, 0.0))
            write(row, value)
        return carry

    lax.fori_loop(0, rows // 8, body, 0, unroll=4)


def slot_of(covering, owner_map, slot):
    position = lax.axis_index("visit")
    residue = lax.rem(position, 4)
    distance = owner_map[covering[0, slot]] - position
    buffer = jnp.int32(0)
    for place, row in enumerate(BUFFER_OF):
        for index, held in enumerate(row):
            here = (residue == place) & (distance == index - len(row) // 2)
            buffer = jnp.where(here, held, buffer)
    return buffer


def near_kernel(table, own, *refs):
    pieces, (out, recip, moved) = refs[:4], refs[4:]
    rows, cols = pieces[0].shape
    blocks = cols // LANES
    slots = moved.shape[0]
    moves = []
    for slot in range(slots):
        held = table[0, slot]
        base, turn, start, masks = shift_of(
            rows, blocks, table[0, slots + slot], table[0, 2 * slots + slot], held <= len(pieces)
        )
        clear_ends(moved.at[slot], rows, blocks)
        for index in range(len(pieces)):

            @pl.when(held == index + 1)
            def _():
                spread(pieces[index], turn, moved.at[slot], base)

        moves.append((moved.at[slot], start, masks))

    def read(row):
        return own[pl.ds(pl.multiple_of(row * blocks, blocks), blocks), :]

    def write(row, value):
        out[row] = value

    add_moved(rows, blocks, read, moves, write)
    column = lax.broadcasted_iota(jnp.int32, (blocks, LANES), 0) * LANES
    column = column + lax.broadcasted_iota(jnp.int32, (blocks, LANES), 1)
    covers = []
    for slot in range(slots):
        source = column - table[0, 2 * slots + slot]
        covers.append(jnp.where((source >= 0) & (source < cols), 1.0, 0.0))

    def cover(step, carry):
        for i in range(8):
            row = step * 8 + i
            total = jnp.ones((blocks, LANES), jnp.float32)
            for slot in range(slots):
                source = row - table[0, slots + slot]
                inside = ((source >= 0) & (source < rows)).astype(jnp.float32)
                total = total + covers[slot] * inside
            recip[row] = 1.0 / total
        return carry

    lax.fori_loop(0, rows // 8, cover, 0, unroll=4)


def relayed_kernel(table, partial, piece, out, moved):
    rows, blocks, _ = partial.shape
    first = table.shape[1] - 6
    valid = table[0, first] > 0
    base, turn, start, masks = shift_of(rows, blocks, table[0, first + 1], table[0, first + 2], valid)

    @pl.when(valid)
    def _():
        clear_ends(moved, rows, blocks)
        spread(piece, turn, moved, base)

    def write(row, value):
        out[row] = value

    add_moved(rows, blocks, lambda row: partial[row], [(moved, start, masks)], write)


def canvas_kernel(
    table, partial, piece, recip, first_rows, last_rows, out, to_inner, to_outer, moved,
):
    rows, blocks, _ = partial.shape
    first = table.shape[1] - 3
    valid = table[0, first] > 0
    base, turn, start, masks = shift_of(rows, blocks, table[0, first + 1], table[0, first + 2], valid)

    @pl.when(valid)
    def _():
        clear_ends(moved, rows, blocks)
        spread(piece, turn, moved, base)

    def write(row, value):
        out[pl.ds(pl.multiple_of(row * blocks, blocks), blocks), :] = value * recip[row]

    add_moved(rows, blocks, lambda row: partial[row], [(moved, start, masks)], write)

    def rows_of(first, count):
        return out[first * blocks : (first + count) * blocks, :].reshape(count, blocks, LANES).astype(jnp.bfloat16)

    edge = to_inner.shape[0] - first_rows.shape[0]
    even = lax.rem(place_of(), 2) == 0
    for message, up in ((to_inner, even), (to_outer, jnp.logical_not(even))):

        @pl.when(up)
        def _():
            message[:edge] = rows_of(0, edge)
            message[edge:] = first_rows[...]

        @pl.when(jnp.logical_not(up))
        def _():
            message[:edge] = rows_of(rows - edge, edge)
            message[edge:] = last_rows[...]


def bands_of(taps, bands):
    count, lanes = taps.shape
    half = lanes // 2
    lower = lax.broadcasted_iota(jnp.int32, (lanes, lanes), 1) < half
    zero = jnp.zeros((lanes, lanes), jnp.float32)

    def table(tap, shift):
        if not 0 <= tap < count:
            return zero
        spread = jnp.broadcast_to(taps[tap : tap + 1, :], (lanes, lanes))
        return pltpu.roll(spread, shift, 1, stride=1, stride_axis=0)

    for offset in range(2 * bands.shape[1]):
        at = slice((offset % 2) * lanes, (offset % 2 + 1) * lanes)
        for pair in range(2):
            plain = table(offset - 2 * pair, 0)
            turned = table(offset - 2 * pair - 1, half)
            to = slice(pair * lanes, (pair + 1) * lanes)
            bands[0, offset // 2, at, to] = jnp.where(lower, plain, turned).astype(bands.dtype)
            bands[1, offset // 2, at, to] = jnp.where(lower, turned, plain).astype(bands.dtype)


def prepare_kernel(
    covering_in, owner_in, row_in, col_in, model_taps, psf_taps, science_in, piece_in,
    table, model_bands, psf_bands, first_rows, last_rows, turned, own,
    covering, owner_map, row_shift, col_shift, science, piece, arrived,
):
    sources = (covering_in, owner_in, row_in, col_in, science_in, piece_in)
    copies = [
        pltpu.make_async_copy(source, target, arrived.at[index])
        for index, (source, target) in enumerate(
            zip(sources, (covering, owner_map, row_shift, col_shift, science, piece))
        )
    ]
    for copy in copies:
        copy.start()
    bands_of(model_taps, model_bands)
    bands_of(psf_taps, psf_bands)
    for copy in copies:
        copy.wait()
    slots = covering.shape[1] - 1
    late = [[jnp.int32(0)] * 3 for _ in range(2)]
    for slot in range(slots):
        held = slot_of(covering, owner_map, slot + 1)
        entry = (held, row_shift[0, slot + 1], col_shift[0, slot + 1])
        for index in range(3):
            table[0, index * slots + slot] = entry[index]
        for buffer in range(2):
            here = held == 5 + buffer
            values = (jnp.int32(1), entry[1], entry[2])
            late[buffer] = [jnp.where(here, new, old) for new, old in zip(values, late[buffer])]
    for buffer in range(2):
        for index in range(3):
            table[0, 3 * (slots + buffer) + index] = late[buffer][index]
    spread(piece, None, own, 0)
    rows, cols = science.shape
    blocks = cols // LANES
    for row in range(0, rows, CHUNK):
        for k in range(blocks):
            at = pl.ds(row * blocks + k, CHUNK, stride=blocks)
            turned[at, :] = science[row : row + CHUNK, k * LANES : (k + 1) * LANES]
    count = first_rows.shape[0] // 2
    for out, first in ((first_rows, 0), (last_rows, rows - count)):
        for row in range(count):
            value = turned[(first + row) * blocks : (first + row + 1) * blocks, :]
            high = value.astype(jnp.bfloat16)
            out[row] = high
            out[count + row] = (value - high.astype(jnp.float32)).astype(jnp.bfloat16)


def pack_rows(source, start, steps, packed, base):
    blocks = 8
    lane = lax.broadcasted_iota(jnp.int32, (blocks, LANES), 1)
    block = lax.broadcasted_iota(jnp.int32, (blocks, LANES), 0)
    inner = block > 0
    outer = block < blocks - 1

    def sides(x):
        at = start + blocks * x
        here = source[at : at + blocks, :]
        before = source[at - 1 : at - 1 + blocks, :]
        after = source[at + 1 : at + 1 + blocks, :]
        return (
            jnp.where(lane < 96, here, jnp.where(inner, before, 0.0)),
            jnp.where(lane >= 32, here, jnp.where(outer, after, 0.0)),
        )

    for phase in range(4):
        last = sides(phase)
        for h in range(1, steps):
            now = sides(4 * h + phase)
            odd, p = (h - 1) % 2, base + (h - 1) // 2
            for side in range(2):
                tile = jnp.concatenate([last[side], now[side]], axis=0).astype(jnp.bfloat16)
                to = slice((phase % 2) * LANES, (phase % 2 + 1) * LANES)
                packed[odd, side, phase // 2, 16 * p : 16 * p + 16, to] = tile
            last = now


def product_of(packed, bands, side, parts):
    chunks = bands.shape[1]
    left = []
    for chunk in range(chunks):
        q, pair = chunk // 2, chunk % 2
        rows = []
        for base, groups in parts:
            first = 16 * (base + q // 2)
            rows.append(packed[q % 2, side, pair, first : first + 8 * groups, :])
        left.append(rows[0] if len(rows) == 1 else jnp.concatenate(rows, axis=0))
    right = bands[side].reshape(chunks * 256, 256)
    return jnp.dot(jnp.concatenate(left, axis=1), right, preferred_element_type=jnp.float32)


def unfold(packed, bands, parts, put):
    low = product_of(packed, bands, 0, parts)
    high = product_of(packed, bands, 1, parts)
    lower = lax.broadcasted_iota(jnp.int32, (8, LANES), 1) < LANES // 2
    for g in range(sum(groups for _, groups in parts)):
        rows = slice(8 * g, 8 * g + 8)
        for pair in range(2):
            lanes = slice(pair * LANES, (pair + 1) * LANES)
            a, b = low[rows, lanes], high[rows, lanes]
            put(4 * g + 2 * pair, jnp.where(lower, a, b))
            put(4 * g + 2 * pair + 1, pltpu.roll(jnp.where(lower, b, a), LANES // 2, 1))


def interior_kernel(rim, psf_rim, canvas, science, model_bands, difference, square, packed):
    blocks = 8
    rows = canvas.shape[0] // blocks
    first = EDGE - psf_rim
    groups = (rows - 2 * first) // 4
    pack_rows(canvas, (first - rim) * blocks, groups + model_bands.shape[1] // 2 - 1, packed, 0)
    totals = [jnp.zeros((blocks, LANES), jnp.float32) for _ in range(4)]

    def put(i, value):
        at = slice((first + i) * blocks, (first + i + 1) * blocks)
        value = science[at, :] - value
        difference[at, :] = value
        totals[i % 4] = totals[i % 4] + value * value

    unfold(packed, model_bands, [(0, groups)], put)
    square[...] = (totals[0] + totals[1]) + (totals[2] + totals[3])


def edge_kernel(
    rim, psf_rim, canvas, inner_rows, outer_rows, science, bands, partial, top, bottom, square, joint, packed,
):
    blocks = 8
    rows = canvas.shape[0] // blocks
    edge = rim + psf_rim
    groups = EDGE // 4
    span = EDGE + 2 * rim
    starts = (blocks, (span + 3) * blocks)
    place = place_of()
    odd = lax.rem(place, 2) == 1
    own = span - edge
    joint[starts[0] + edge * blocks : starts[0] + span * blocks, :] = canvas[: own * blocks, :]
    joint[starts[1] : starts[1] + own * blocks, :] = canvas[(rows - own) * blocks :, :]
    for swapped in range(2):

        @pl.when(odd == (swapped == 1))
        def _():
            above, below = (outer_rows, inner_rows) if swapped else (inner_rows, outer_rows)
            to = starts[0]
            joint[to : to + edge * blocks, :] = above[:edge].astype(jnp.float32).reshape(-1, LANES)
            to = starts[1] + own * blocks
            joint[to : to + edge * blocks, :] = below[:edge].astype(jnp.float32).reshape(-1, LANES)
            for source, at in ((above, 0), (below, psf_rim)):
                value = source[edge : edge + psf_rim].astype(jnp.float32)
                value = value + source[edge + psf_rim : edge + 2 * psf_rim].astype(jnp.float32)
                to = (2 * (span + 3) + at) * blocks
                joint[to : to + psf_rim * blocks, :] = value.reshape(-1, LANES)

    steps = groups + bands.shape[1] // 2 - 1
    pairs = steps // 2
    pack_rows(joint, starts[0], steps, packed, 0)
    pack_rows(joint, starts[1], steps, packed, pairs)
    totals = [partial[...], jnp.zeros((blocks, LANES), jnp.float32)]

    def put(i, value):
        side, row = i // EDGE, i % EDGE
        target = (top, bottom)[side]
        at = slice(row * blocks, (row + 1) * blocks)
        outside = row < psf_rim if side == 0 else row >= EDGE - psf_rim
        if outside:
            which = row if side == 0 else psf_rim + row - (EDGE - psf_rim)
            to = (2 * (span + 3) + which) * blocks
            joined = place > 0 if side == 0 else place < PIECES - 1
            target[at, :] = jnp.where(joined, joint[to : to + blocks, :] - value, 0.0)
        else:
            to = (row - psf_rim if side == 0 else rows - EDGE + psf_rim + row) * blocks
            value = science[to : to + blocks, :] - value
            target[at, :] = value
            totals[side] = totals[side] + value * value

    unfold(packed, bands, [(0, groups), (pairs, groups)], put)
    square[...] = jnp.broadcast_to(jnp.sum(totals[0] + totals[1]), square.shape)


def rest_kernel(psf_rim, top, bottom, inside, bands, difference, response, joint, packed):
    blocks = 8
    rows, _ = difference.shape
    start = blocks
    more = rows + 2 * psf_rim - 2 * EDGE
    first = start + EDGE * blocks
    joint[start:first, :] = top[...]
    from_row = EDGE - psf_rim
    joint[first : first + more * blocks, :] = inside[from_row * blocks : (from_row + more) * blocks, :]
    joint[first + more * blocks : first + (more + EDGE) * blocks, :] = bottom[...]
    groups = rows // 4
    pack_rows(joint, start, groups + bands.shape[1] // 2 - 1, packed, 0)

    def put(i, value):
        response[i * blocks : (i + 1) * blocks, :] = value

    unfold(packed, bands, [(0, groups)], put)
    for row in range(0, rows, 8):
        for k in range(blocks):
            at = pl.ds(start + (row + psf_rim) * blocks + k, 8, stride=blocks)
            difference[row : row + 8, k * LANES : (k + 1) * LANES] = joint[at, :]


def detection_kernel(count, response, *refs):
    out = refs[-1]
    total = refs[0][...]
    for ref in refs[1:-1]:
        total = total + ref[...]
    scale = 1.0 / jnp.sqrt(total / count + 1e-06)
    rows, cols = out.shape
    blocks = cols // LANES
    first = pl.multiple_of(pl.program_id(0) * (rows * blocks), rows * blocks)
    for row in range(0, rows, 8):
        for k in range(blocks):
            at = pl.ds(first + row * blocks + k, 8, stride=blocks)
            out[row : row + 8, k * LANES : (k + 1) * LANES] = response[at, :] * scale


def tap_rows(taps, width):
    rim = taps.shape[1] // 2
    turned = jnp.flip(taps, axis=1)
    gap = jnp.zeros((taps.shape[0], width - taps.shape[1]), jnp.float32)
    return jnp.concatenate([turned[:, rim:], gap, turned[:, :rim]], axis=1)


def shards(
    science,
    template,
    owner_map,
    covering,
    row_shift,
    col_shift,
    basis_cols,
    basis_rows,
    coeffs,
    psf_kernel,
):
    image_rows, image_cols = science.shape
    devices = lax.axis_size("visit")
    position = lax.axis_index("visit")
    held_piece = (position + 1) % devices
    visit_id = held_piece // PIECES
    slot_count = covering.shape[1]
    rim = basis_cols.shape[1] // 2
    psf_rim = psf_kernel.shape[0] // 2
    blocks = image_cols // LANES
    vmem = pl.BlockSpec(memory_space=pltpu.VMEM)
    smem = pl.BlockSpec(memory_space=pltpu.SMEM)
    in_hbm = pl.BlockSpec(memory_space=pltpu.HBM)

    pieces = gather_pieces(template)

    coeff_row = lax.dynamic_index_in_dim(coeffs, visit_id, 0, keepdims=False)
    weights = (coeff_row[:, None] * basis_rows).astype(jnp.bfloat16)
    model_taps = jnp.einsum(
        "bs,bt->st", weights, basis_cols.astype(jnp.bfloat16), preferred_element_type=jnp.float32
    )
    psf_taps = psf_kernel.astype(jnp.bfloat16).astype(jnp.float32)
    model_chunks = (basis_rows.shape[1] + 3) // 2
    psf_chunks = (psf_kernel.shape[0] + 3) // 2
    edge = rim + psf_rim
    sent = jax.ShapeDtypeStruct((edge + 2 * psf_rim, blocks, LANES), jnp.bfloat16)
    rim_rows = jax.ShapeDtypeStruct((2 * psf_rim, blocks, LANES), jnp.bfloat16)
    turned_shape = jax.ShapeDtypeStruct((image_rows * blocks, LANES), jnp.float32)
    table, model_bands, psf_bands, first_rows, last_rows, turned, own = pl.pallas_call(
        prepare_kernel,
        out_shape=(
            jax.ShapeDtypeStruct((1, 3 * (slot_count + 1)), jnp.int32),
            jax.ShapeDtypeStruct((2, model_chunks, 256, 256), jnp.bfloat16),
            jax.ShapeDtypeStruct((2, psf_chunks, 256, 256), jnp.bfloat16),
            rim_rows,
            rim_rows,
            turned_shape,
            turned_shape,
        ),
        in_specs=[in_hbm] * 4 + [vmem] * 2 + [in_hbm] * 2,
        out_specs=(smem,) + (vmem,) * 6,
        scratch_shapes=[
            pltpu.SMEM(covering.shape, jnp.int32),
            pltpu.SMEM(owner_map.shape, jnp.int32),
            pltpu.SMEM(row_shift.shape, jnp.int32),
            pltpu.SMEM(col_shift.shape, jnp.int32),
            pltpu.VMEM(science.shape, science.dtype),
            pltpu.VMEM(template.shape, template.dtype),
            pltpu.SemaphoreType.DMA((6,)),
        ],
        compiler_params=pltpu.CompilerParams(vmem_limit_bytes=16 * 2**20),
        cost_estimate=cost(4),
        name="prepare",
    )(
        covering, owner_map, row_shift, col_shift,
        tap_rows(model_taps, LANES), tap_rows(psf_taps, LANES), science, template,
    )

    moved_rows = (2 * image_rows + 3) * blocks
    canvas_shape = jax.ShapeDtypeStruct((image_rows, blocks, LANES), jnp.float32)
    moved = pltpu.VMEM((moved_rows, LANES), jnp.float32)
    partial, recip = pl.pallas_call(
        near_kernel,
        out_shape=(canvas_shape, canvas_shape),
        in_specs=[smem] + [vmem] * 5,
        out_specs=(vmem, vmem),
        scratch_shapes=[
            pltpu.VMEM((slot_count - 1, moved_rows, LANES), jnp.float32),
        ],
        compiler_params=pltpu.CompilerParams(vmem_limit_bytes=20 * 2**20),
        cost_estimate=cost(11),
        name="near",
    )(table, own, *pieces[1:5])
    partial = pl.pallas_call(
        relayed_kernel,
        out_shape=canvas_shape,
        in_specs=[smem] + [vmem] * 2,
        out_specs=vmem,
        scratch_shapes=[moved],
        compiler_params=pltpu.CompilerParams(vmem_limit_bytes=12 * 2**20),
        cost_estimate=cost(5),
        name="relayed",
    )(table, partial, pieces[5])
    canvas, to_inner, to_outer = pl.pallas_call(
        canvas_kernel,
        out_shape=(turned_shape, sent, sent),
        in_specs=[smem] + [vmem] * 5,
        out_specs=(vmem, vmem, vmem),
        scratch_shapes=[moved],
        compiler_params=pltpu.CompilerParams(vmem_limit_bytes=12 * 2**20),
        cost_estimate=cost(5),
        name="canvas",
    )(table, partial, pieces[6], recip, first_rows, last_rows)

    groups = [[(first + i - 1) % devices for i in range(PIECES)] for first in range(0, devices, PIECES)]

    def swap(value, pairs):
        return lax.ppermute(value, "visit", [(g[a], g[b]) for g in groups for a, b in pairs])

    inner_rows = swap(to_inner, [(1, 2), (2, 1)])
    outer_rows = swap(to_outer, [(0, 1), (1, 0), (2, 3), (3, 2)])

    square_shape = jax.ShapeDtypeStruct((8, LANES), jnp.float32)
    inside, inside_square = pl.pallas_call(
        lambda *refs: interior_kernel(rim, psf_rim, *refs),
        out_shape=(turned_shape, square_shape),
        in_specs=[vmem] * 3,
        out_specs=(vmem, vmem),
        scratch_shapes=[pltpu.VMEM((2, 2, 2, (image_rows // 8 + 2) * 16, 256), jnp.bfloat16)],
        compiler_params=pltpu.CompilerParams(vmem_limit_bytes=16 * 2**20),
        cost_estimate=cost(7),
        name="interior",
    )(canvas, turned, model_bands)
    end_shape = jax.ShapeDtypeStruct((EDGE * blocks, LANES), jnp.float32)
    top, bottom, square = pl.pallas_call(
        lambda *refs: edge_kernel(rim, psf_rim, *refs),
        out_shape=(end_shape, end_shape, square_shape),
        in_specs=[vmem] * 6,
        out_specs=(vmem, vmem, vmem),
        scratch_shapes=[
            pltpu.VMEM(((2 * (EDGE + 2 * rim + 3) + 2 * psf_rim) * blocks, LANES), jnp.float32),
            pltpu.VMEM((2, 2, 2, (EDGE // 4 + model_chunks) * 16, 256), jnp.bfloat16),
        ],
        compiler_params=pltpu.CompilerParams(vmem_limit_bytes=16 * 2**20),
        cost_estimate=cost(4),
        name="edge",
    )(canvas, inner_rows, outer_rows, turned, model_bands, inside_square)

    totals = [square]
    for turn in SUMS:
        if isinstance(turn, int):
            links = [(g[i], g[(i + turn) % PIECES]) for g in groups for i in range(PIECES)]
        else:
            links = [(g[a], g[b]) for g in groups for p in turn for a, b in (p, p[::-1])]
        totals.append(lax.ppermute(square, "visit", links))

    difference, response = pl.pallas_call(
        lambda *refs: rest_kernel(psf_rim, *refs),
        out_shape=(jax.ShapeDtypeStruct((image_rows, image_cols), jnp.float32), turned_shape),
        in_specs=[vmem] * 4,
        out_specs=(vmem, vmem),
        scratch_shapes=[
            pltpu.VMEM(((image_rows + 2 * psf_rim + 3) * blocks, LANES), jnp.float32),
            pltpu.VMEM((2, 2, 2, (image_rows // 8 + 2) * 16, 256), jnp.bfloat16),
        ],
        compiler_params=pltpu.CompilerParams(vmem_limit_bytes=16 * 2**20),
        cost_estimate=cost(8),
        name="rest",
    )(top, bottom, inside, psf_bands)
    count = float(PIECES * image_rows * image_cols)
    detection = pl.pallas_call(
        lambda *refs: detection_kernel(count, *refs),
        out_shape=jax.ShapeDtypeStruct((image_rows, image_cols), jnp.float32),
        grid=(STEPS,),
        in_specs=[vmem] * (1 + PIECES),
        out_specs=pl.BlockSpec((image_rows // STEPS, image_cols), lambda i: (i, 0)),
        compiler_params=pltpu.CompilerParams(vmem_limit_bytes=8 * 2**20),
        cost_estimate=cost(4),
        name="detection",
    )(response, *totals)
    return (difference, detection)


def solution(mesh):
    return jax.shard_map(
        shards,
        mesh=mesh,
        in_specs=(
            P(("groups", "visit"), None),
            P(("groups", "visit"), None),
            P("groups"),
            P(("groups", "visit"), None),
            P(("groups", "visit"), None),
            P(("groups", "visit"), None),
            P(),
            P(),
            P("groups", None),
            P(),
        ),
        out_specs=(P(("groups", "visit"), None), P(("groups", "visit"), None)),
        check_vma=False,
    )
```
